256 devices in a mesh: space: 16 (over z, x_hi), mrow: 4 (over y), mcol: 4 (over x_lo, core).
Axes of the slice: x: 4 (x_hi: 2, x_lo: 2; x = x_hi * 2 + x_lo), y: 4, z: 8, core: 2. Of those that a mesh axis runs over, the one named last changes fastest.
Arguments:
- deviation: bfloat16 [512, 48, 8192], P('space', None, ('mcol', 'mrow'))
- courant: float32 [2, 8192], P(None, ('mcol', 'mrow')), may hold values from -0.95 to 0.95
- collide: bfloat16 [8192, 8192], P('mrow', ('mcol', 'space'))
- hole_cells: int32 [6144], P('space'), may hold values from -1 to 1535, as said below
- hole_wall: int32 [6144], P('space'), may hold values from 0 to 3
- specular: int32 [4, 8192], replicated, may hold values from 0 to 8191, as said below
- specularity: float32 [4], replicated, may hold values from 0.2 to 0.8
Outputs:
- updated: bfloat16 [512, 48, 8192], P('space', None, ('mrow', 'mcol'))
The draws below stay inside these ranges and needn't reach their ends.
Inputs may be any that keep to these rules, and one draw needn't show every extreme that they name: `hole_cells`: within one tile the used slots come first and name distinct cells; every tile has at least 96 used slots, some tile has all 384 slots used and some tile has an empty slot. Each row specular[w] is a permutation of the modes; for an outgoing mode i of aligned block e = i // 512, its incoming mode j lies, within j's own aligned block of 512 modes, in the sub-block of 32 modes numbered e, that is (j % 512) // 32 == e.
All inputs are finite; a program needn't handle non-finite values.
Results may differ from the reference program's by a relative error of at most 0.005.
Values may be sent and summed in bfloat16 or wider, within the bound.
A program may use at most 128 MiB of HBM per device.

```python
import math
import jax
import jax.numpy as jnp
from jax import lax

M = 8192
NW = 4
CX = 32
CY = 48
BMAX = 384
NX = 512
N_SPACE = 16
N_MROW = 4
N_MCOL = 4


def draw_deviation(key, part):
    key_off, key_noise, key_scale = jax.random.split(key, 3)
    offset = jax.random.uniform(key_off, (NX, CY, 1), jnp.float32, -1.0, 1.0)
    scales = jnp.exp(jax.random.uniform(key_scale, (1, 1, M), jnp.float32, math.log(0.3), math.log(3.0)))
    noise = jnp.clip(jax.random.normal(key_noise, (NX, CY, M), jnp.float32), -4.0, 4.0)
    return (offset + scales * noise).astype(jnp.bfloat16)


def draw_collide(key, part):
    key_off, key_diag = jax.random.split(key, 2)
    spread = 0.5 * jnp.clip(jax.random.normal(key_off, (M, M), jnp.float32), -4.0, 4.0) / math.sqrt(M)
    diagonal = jax.random.uniform(key_diag, (M, 1), jnp.float32, 0.3, 0.9)
    row_ids = jnp.arange(M, dtype=jnp.int32)[:, None]
    col_ids = jnp.arange(M, dtype=jnp.int32)[None, :]
    return jnp.where(row_ids == col_ids, diagonal, spread).astype(jnp.bfloat16)


def draw_hole_cells(key, part):
    key_perm, key_count, key_pick, key_slot = jax.random.split(key, 4)
    tile_cells = CX * CY
    tile_keys = jax.random.split(key_perm, N_SPACE)
    orders = jax.vmap(lambda single: jax.random.permutation(single, tile_cells - 1))(tile_keys)[:, :BMAX]
    forced = jax.random.randint(key_pick, (), 0, N_SPACE)
    chosen_slot = jax.random.randint(key_slot, (), 0, BMAX)
    slot_ids = jnp.arange(BMAX, dtype=jnp.int32)
    tile_ids = jnp.arange(N_SPACE, dtype=jnp.int32)
    orders = jnp.where((tile_ids[:, None] == forced) & (slot_ids[None, :] == chosen_slot), tile_cells - 1, orders)
    counts = jax.random.randint(key_count, (N_SPACE,), BMAX // 4, BMAX)
    counts = jnp.where(tile_ids == forced, BMAX, counts)
    return jnp.where(slot_ids[None, :] < counts[:, None], orders, -1).reshape(-1).astype(jnp.int32)


def draw_specular(key, part):
    groups = N_MROW * N_MCOL
    block = M // groups
    sub = block // groups
    key_shift, key_off = jax.random.split(jax.random.fold_in(key, 17))
    shift_keys = jax.random.split(key_shift, NW)
    sigma = jax.vmap(lambda single: jax.random.permutation(single, groups))(shift_keys).astype(jnp.int32)
    offsets = jax.random.randint(key_off, (NW, groups, groups), 0, sub).astype(jnp.int32)
    modes = jnp.arange(M, dtype=jnp.int32)
    dest_block = modes // block
    sub_index = modes % block // sub
    within = modes % sub
    source_block = (dest_block[None, :] + sigma[:, sub_index]) % groups
    source_within = (within[None, :] + offsets[:, dest_block, sub_index]) % sub
    return (source_block * block + dest_block[None, :] * sub + source_within).astype(jnp.int32)


def place_ends(values, own_key, least, top_value):
    dims = values.shape
    index_at = [jax.random.randint(jax.random.fold_in(own_key, axis), (), 0, dims[axis]) for axis in range(len(dims))]
    values = values.at[tuple(index_at)].set(least)
    longest = dims.index(max(dims))
    index_at[longest] = (index_at[longest] + 1) % dims[longest]
    return values.at[tuple(index_at)].set(top_value)


def steps_of(key, extent, pieces, smallest, high):
    def one(axis_at, blocks):
        steps = jax.random.uniform(jax.random.fold_in(jax.random.fold_in(key, 6), axis_at), (blocks,), jnp.float32, smallest / len(pieces), high / len(pieces))
        return jnp.repeat(jnp.exp(steps), extent[axis_at] // blocks).reshape((-1,) + (1,) * (len(extent) - axis_at - 1))

    level = one(*pieces[0])
    for cut in pieces[1:]:
        level = level * one(*cut)
    return level


def setup_inputs(seed: int = 0) -> dict:
    streams_of = jax.random.split(jax.random.key(seed), 8)
    deviation = draw_deviation(jax.random.fold_in(streams_of[7], 71), 0)
    courant = jnp.clip(jax.random.uniform(streams_of[1], (2, M), jnp.float32, -0.95, 0.95) * steps_of(streams_of[1], (2, M), ((1, 16),), -0.4, 0.0), -0.95, 0.95)
    collide = draw_collide(jax.random.fold_in(streams_of[7], 71), 0)
    hole_cells = draw_hole_cells(jax.random.fold_in(streams_of[7], 71), 0)
    hole_wall = place_ends(jax.random.randint(streams_of[4], (N_SPACE * BMAX,), 0, NW), jax.random.fold_in(streams_of[4], 1), 0, NW - 1).astype(jnp.int32)
    specular = draw_specular(jax.random.fold_in(streams_of[7], 71), 0)
    specularity = jnp.clip(jax.random.uniform(streams_of[6], (NW,), jnp.float32, 0.2, 0.8), 0.2, 0.8)
    return dict(deviation=deviation, courant=courant, collide=collide, hole_cells=hole_cells, hole_wall=hole_wall, specular=specular, specularity=specularity)


def upwind(padded, courant):
    field = padded.astype(jnp.float32)
    reach_x = jnp.abs(courant[0])
    reach_y = jnp.abs(courant[1])
    center = field[1:-1]
    upwind_x = jnp.where(courant[0] > 0, field[:-2], field[2:])
    upwind_y = jnp.where(courant[1] > 0, jnp.roll(center, 1, axis=1), jnp.roll(center, -1, axis=1))
    upwind_xy = jnp.where(courant[1] > 0, jnp.roll(upwind_x, 1, axis=1), jnp.roll(upwind_x, -1, axis=1))
    result = (1.0 - reach_x) * (1.0 - reach_y) * center + reach_x * (1.0 - reach_y) * upwind_x
    result = result + (1.0 - reach_x) * reach_y * upwind_y + reach_x * reach_y * upwind_xy
    return result.astype(jnp.bfloat16)


def reference(deviation, courant, collide, hole_cells, hole_wall, specular, specularity):
    length_x, width_y, modes = deviation.shape
    block_len = min(512, modes)
    block_count = modes // block_len
    blocks = deviation.reshape(length_x, width_y, block_count, block_len).transpose(2, 0, 1, 3)
    speeds = courant.reshape(2, block_count, block_len).transpose(1, 0, 2)

    def stream_block(pair):
        part_dev, part_speed = pair
        padded = jnp.pad(part_dev, ((1, 1), (0, 0), (0, 0)))
        return upwind(padded, part_speed)

    read = lax.map(stream_block, (blocks, speeds))
    read = read.transpose(1, 2, 0, 3).reshape(length_x * width_y, modes)
    tile_cells = CX * CY
    tile_ids = jnp.arange(hole_cells.shape[0], dtype=jnp.int32) // BMAX
    is_live = hole_cells >= 0
    global_ids = jnp.where(is_live, tile_ids * tile_cells + hole_cells, 0).astype(jnp.int32)
    rim_rows = read[global_ids]
    diffuse = jnp.sum(rim_rows.astype(jnp.float32), axis=1) / modes
    source_modes = specular[hole_wall]
    mirrored = jnp.take_along_axis(rim_rows, source_modes, axis=1).astype(jnp.float32)
    share = specularity[hole_wall][:, None]
    emitted = (share * mirrored + (1.0 - share) * diffuse[:, None]).astype(jnp.bfloat16)
    target_ids = jnp.where(is_live, global_ids, length_x * width_y).astype(jnp.int32)
    reemitted = read.at[target_ids].set(emitted, mode="drop")
    product = lax.dot_general(reemitted, collide, (((1,), (1,)), ((), ())), preferred_element_type=jnp.float32)
    return product.astype(jnp.bfloat16).reshape(length_x, width_y, modes)
```

```python
import functools

import jax
import jax.numpy as jnp
from jax import lax
from jax.experimental import pallas as pl
from jax.experimental.pallas import tpu as pltpu
from jax.sharding import PartitionSpec as P

MESH = pl.DeviceIdType.MESH
F32 = jnp.float32
BF16 = jnp.bfloat16
CHUNKS = 4


def column_of(row, slots):
    return jnp.broadcast_to(row, (128, slots)).T


def widen(tile, count):
    return jnp.concatenate([tile] * count, axis=1)


def body(
    sizes,
    dev_ref,
    cour_ref,
    coll_ref,
    cells_ref,
    wall_ref,
    spec_ref,
    share_ref,
    out_ref,
    cols,
    mats,
    read_buf,
    halo,
    msg_out,
    msg_in,
    pair_out,
    pair_in,
    chip_out,
    chip_in,
    z_send,
    z_recv,
    x_send,
    x_recv,
    halo_send,
    halo_recv,
    msg_send,
    msg_recv,
    y_send,
    y_recv,
    pair_send,
    pair_recv,
    chip_send,
    chip_recv,
    own_sem,
):
    n_space, n_row, n_col = sizes
    depth = n_space // 2
    width_x, width_y, block = dev_ref.shape
    cells = width_x * width_y
    slots = cells_ref.shape[1]
    walls, modes = spec_ref.shape
    groups = n_row * n_col
    sub = block // groups
    chunk = cells // CHUNKS
    far = depth // 2
    half = block // 2

    s = lax.axis_index("space")
    y = lax.axis_index("mrow")
    q = lax.axis_index("mcol")
    z, h = s // 2, s % 2
    l, c = q // 2, q % 2
    mate_s = z * 2 + (1 - h)
    z_next = (s + 2) % n_space
    z_prev = (s + n_space - 2) % n_space
    other_s = (s + 2 * h - 1 + n_space) % n_space
    s_next = (s + 1) % n_space
    s_prev = (s + n_space - 1) % n_space
    y_next = (y + 1) % n_row
    y_prev = (y + n_row - 1) % n_row
    core_q = l * 2 + (1 - c)
    chip_q = (1 - l) * 2 + c
    blocks = (
        (1 - l) * 2 + (1 - c),
        (1 - l) * 2 + c,
        l * 2 + (1 - c),
        l * 2 + c,
    )
    mine = q * n_row + y

    peers = []
    for dq in range(n_col):
        for dy in range(n_row):
            if dq or dy:
                peers.append(((y + dy) % n_row, (q + dq) % n_col))

    barrier = pltpu.get_barrier_semaphore()
    for target in (z_next, z_prev, mate_s, other_s):
        pl.semaphore_signal(barrier, inc=1, device_id=(target, y, q), device_id_type=MESH)
    for ty, tq in peers:
        pl.semaphore_signal(barrier, inc=1, device_id=(s, ty, tq), device_id_type=MESH)
    pl.semaphore_wait(barrier, 4 + len(peers))

    started = []

    def remote(src, dst, send, recv, target):
        return pltpu.make_async_remote_copy(
            src_ref=src,
            dst_ref=dst,
            send_sem=send,
            recv_sem=recv,
            device_id=target,
            device_id_type=MESH,
        )

    def go(copy):
        copy.start()
        started.append(copy)

    def rows_of(turn, offset=0, size=None):
        size = block if size is None else size
        return pl.ds(pl.multiple_of(blocks[turn] * block + offset, size), size)

    def z_copy(way, group, hop, piece):
        turn = group * 2 + piece % 2
        if way == 0:
            source = (z + depth - (hop - 1)) % depth
            target = z_next
        else:
            source = (z + hop - 1) % depth
            target = z_prev
        slot = source * 2 + (h if piece < 2 else 1 - h)
        if hop == far:
            rows = rows_of(turn, way * half, half)
        else:
            rows = rows_of(turn)
        index = ((way * 2 + group) * far + hop - 1) * 4 + piece
        dst = mats.at[slot, rows]
        src = coll_ref.at[rows] if hop == 1 and piece < 2 else dst
        return remote(src, dst, z_send.at[index], z_recv.at[index], (target, y, q))

    def z_start(group, hop, pieces):
        for piece in pieces:
            for way in range(2):
                go(z_copy(way, group, hop, piece))

    def z_serve(group, hop, pieces):
        for piece in pieces:
            for way in range(2):
                z_copy(way, group, hop, piece).wait_recv()
                if hop < far:
                    go(z_copy(way, group, hop + 1, piece))

    def x_copy(turn):
        rows = rows_of(turn)
        return remote(
            coll_ref.at[rows],
            mats.at[s, rows],
            x_send.at[turn],
            x_recv.at[turn],
            (mate_s, y, q),
        )

    def y_copy(way, stage, part):
        target = y_next if way == 0 else y_prev
        if stage == 0:
            owner = y
            rows = pl.ds(part * chunk, chunk)
        else:
            owner = y_prev if way == 0 else y_next
            rows = pl.ds(part * chunk + way * (chunk // 2), chunk // 2)
        index = (way * 2 + stage) * CHUNKS + part
        ref = cols.at[owner, rows]
        return remote(ref, ref, y_send.at[index], y_recv.at[index], (s, target, q))

    def y_start(part):
        for way in range(2):
            go(y_copy(way, 0, part))

    def y_forward(part):
        for way in range(2):
            y_copy(way, 0, part).wait_recv()
            go(y_copy(way, 1, part))

    def y_finish(part):
        for way in range(2):
            y_copy(way, 1, part).wait_recv()

    def pair_copy(stage, part):
        rows = pl.ds(part * chunk, chunk)
        index = stage * CHUNKS + part
        return remote(
            pair_out.at[stage, rows],
            pair_in.at[stage, rows],
            pair_send.at[index],
            pair_recv.at[index],
            (s, y, core_q),
        )

    def chip_copy(part):
        rows = pl.ds(part * chunk, chunk)
        return remote(
            chip_out.at[rows],
            chip_in.at[rows],
            chip_send.at[part],
            chip_recv.at[part],
            (s, y, chip_q),
        )

    def product(turn, part):
        rows = pl.ds(part * chunk, chunk)
        total = None
        per = block // mats.shape[2]
        for owner in range(n_row):
            right = jnp.concatenate(
                [mats[owner * per + step, rows_of(turn), :] for step in range(per)], axis=1
            )
            term = lax.dot_general(
                cols[owner, rows, :],
                right,
                (((1,), (1,)), ((), ())),
                preferred_element_type=F32,
            )
            total = term if total is None else total + term
        return total

    halo_up = remote(
        dev_ref.at[width_x - 1], halo.at[0], halo_send.at[0], halo_recv.at[0], (s_next, y, q)
    )
    halo_down = remote(dev_ref.at[0], halo.at[1], halo_send.at[1], halo_recv.at[1], (s_prev, y, q))
    go(halo_up)
    go(halo_down)
    x_copies = [x_copy(turn) for turn in range(4)]
    go(x_copies[0])
    go(x_copies[1])
    z_start(0, 1, (0, 1))
    own_copy = pltpu.make_async_copy(coll_ref, mats.at[s], own_sem)
    own_copy.start()

    reach_x = jnp.abs(cour_ref[0:1, :])
    reach_y = jnp.abs(cour_ref[1:2, :])
    forward_x = cour_ref[0:1, :] > 0
    forward_y = cour_ref[1:2, :] > 0

    def stream(center, before, after):
        mixed = (1.0 - reach_x) * center + reach_x * jnp.where(forward_x, before, after)
        shifted = jnp.where(
            forward_y, pltpu.roll(mixed, 1, 0), pltpu.roll(mixed, width_y - 1, 0)
        )
        return ((1.0 - reach_y) * mixed + reach_y * shifted).astype(BF16)

    def layer(index):
        return dev_ref[index].astype(F32)

    @pl.loop(1, width_x - 1)
    def _(x):
        rows = pl.ds(pl.multiple_of(x * width_y, width_y), width_y)
        read_buf[rows, :] = stream(layer(x), layer(x - 1), layer(x + 1))

    halo_up.wait_recv()
    halo_down.wait_recv()
    low = jnp.where(s == 0, 0.0, halo[0].astype(F32))
    high = jnp.where(s == n_space - 1, 0.0, halo[1].astype(F32))
    read_buf[pl.ds(0, width_y), :] = stream(layer(0), low, layer(1))
    read_buf[pl.ds(cells - width_y, width_y), :] = stream(
        layer(width_x - 1), layer(width_x - 2), high
    )

    x_copies[0].wait_recv()
    x_copies[1].wait_recv()
    z_start(0, 1, (2, 3))

    cells_row = cells_ref[...].astype(F32)
    cells_col = column_of(cells_row, slots)
    lane = lax.broadcasted_iota(jnp.int32, (slots, 128), 1).astype(F32)
    pick = jnp.concatenate(
        [
            jnp.where(cells_col == lane + float(base), 1.0, 0.0).astype(BF16)
            for base in range(0, cells, 128)
        ],
        axis=1,
    )
    rim = jnp.dot(pick, read_buf[...], preferred_element_type=F32).T
    partial = jnp.sum(rim, axis=0, keepdims=True)
    first = partial.astype(BF16).astype(F32)
    second = (partial - first).astype(BF16).astype(F32)
    third = partial - first - second
    line = lax.broadcasted_iota(jnp.int32, (16, slots), 0)
    stats = jnp.where(
        line == 0, first, jnp.where(line == 1, second, jnp.where(line == 2, third, 0.0))
    ).astype(BF16)
    for e in range(groups):
        msg_out[e, 0:sub, :] = rim[e * sub : (e + 1) * sub].astype(BF16)
        msg_out[e, sub : sub + 16, :] = stats
    msg_copies = []
    for index, (ty, tq) in enumerate(peers):
        copy = remote(
            msg_out.at[tq * n_row + ty],
            msg_in.at[mine],
            msg_send.at[index],
            msg_recv.at[index],
            (s, ty, tq),
        )
        go(copy)
        msg_copies.append(copy)
    msg_in[mine] = msg_out[mine]
    go(x_copies[2])
    go(x_copies[3])

    z_serve(0, 1, (0, 1, 2))

    wall_col = column_of(wall_ref[...].astype(F32), slots)
    table = spec_ref[:, pl.ds(pl.multiple_of(mine * block, block), block)]
    place = (table // block) * sub + table % sub
    share = jnp.zeros((slots, 128), F32)
    for w in range(walls):
        share = jnp.where(wall_col == float(w), share_ref[w], share)

    for copy in msg_copies:
        copy.wait_recv()
    received = msg_in[...].astype(F32)
    inner = received[:, 0:sub, :].reshape(groups * sub, slots).T
    diffuse = jnp.sum(jnp.sum(received[:, sub : sub + 16, :], axis=0), axis=0, keepdims=True)
    diffuse = widen(column_of(diffuse / modes, slots), block // 128)
    spot = lax.broadcasted_iota(jnp.int32, (groups * sub, block), 0)
    mirrored = None
    for w in range(walls):
        chosen = jnp.where(widen(wall_col == float(w), block // 128), inner, 0.0).astype(BF16)
        route = jnp.where(spot == place[w : w + 1, :], 1.0, 0.0).astype(BF16)
        term = jnp.dot(chosen, route, preferred_element_type=F32)
        mirrored = term if mirrored is None else mirrored + term
    share = widen(share, block // 128)
    emitted = (share * mirrored + (1.0 - share) * diffuse).astype(BF16)
    emitted = jnp.concatenate([emitted, jnp.ones((slots, 128), BF16)], axis=1)

    spread = jnp.broadcast_to(cells_row, (chunk, slots))
    cell_of = lax.broadcasted_iota(jnp.int32, (chunk, slots), 0).astype(F32)

    def patch(part):
        rows = pl.ds(part * chunk, chunk)
        place_at = jnp.where(spread == cell_of + float(part * chunk), 1.0, 0.0).astype(BF16)
        placed = jnp.dot(place_at, emitted, preferred_element_type=F32)
        hole = widen(placed[:, block:], block // 128) > 0.5
        cols[y, rows, :] = jnp.where(
            hole, placed[:, :block], read_buf[rows, :].astype(F32)
        ).astype(BF16)

    patch(0)
    y_start(0)
    patch(1)
    y_start(1)
    patch(2)
    patch(3)

    z_serve(0, 1, (3,))
    z_serve(0, 2, (0, 1, 2, 3))
    y_forward(0)
    y_start(2)
    z_serve(0, 3, (0, 1))
    y_forward(1)
    y_start(3)
    z_serve(0, 3, (2, 3))
    x_copies[2].wait_recv()
    x_copies[3].wait_recv()
    z_start(1, 1, (0, 1, 2, 3))
    z_serve(0, 4, (0, 1, 2, 3))
    own_copy.wait()

    def pass_on(part):
        rows = pl.ds(part * chunk, chunk)
        pair_out[0, rows, :] = product(0, part)
        go(pair_copy(0, part))
        total = product(1, part)
        pair_copy(0, part).wait_recv()
        chip_out[rows, :] = (total + pair_in[0, rows, :]).astype(BF16)
        go(chip_copy(part))

    y_finish(0)
    pass_on(0)
    y_forward(2)
    z_serve(1, 1, (0, 1))
    y_finish(1)
    pass_on(1)
    z_serve(1, 1, (2, 3))
    y_forward(3)
    z_serve(1, 2, (0, 1, 2, 3))
    y_finish(2)
    pass_on(2)
    y_finish(3)
    pass_on(3)
    z_serve(1, 3, (0, 1, 2, 3))
    z_serve(1, 4, (0, 2))
    for part in range(CHUNKS):
        rows = pl.ds(part * chunk, chunk)
        pair_out[1, rows, :] = product(2, part)
        go(pair_copy(1, part))
    z_serve(1, 4, (1, 3))
    for part in range(CHUNKS):
        rows = pl.ds(part * chunk, chunk)
        total = product(3, part)
        pair_copy(1, part).wait_recv()
        chip_copy(part).wait_recv()
        out_ref[rows, :] = (
            total + pair_in[1, rows, :] + chip_in[rows, :].astype(F32)
        ).astype(BF16)
    for copy in started:
        copy.wait_send()


def on_device(sizes, deviation, courant, collide, hole_cells, hole_wall, specular, specularity):
    width_x, width_y, block = deviation.shape
    cells = width_x * width_y
    n_space, n_row, n_col = sizes
    groups = n_row * n_col
    slots = hole_cells.shape[0]
    rows, piece = collide.shape
    vmem = pl.BlockSpec(memory_space=pltpu.VMEM)
    smem = pl.BlockSpec(memory_space=pltpu.SMEM)
    dma = pltpu.SemaphoreType.DMA
    hops = 2 * 2 * (n_space // 4) * 4
    ways = 2 * 2 * CHUNKS
    sub = block // groups
    result = pl.pallas_call(
        functools.partial(body, sizes),
        out_shape=jax.ShapeDtypeStruct((cells, block), BF16),
        in_specs=[vmem] * 6 + [smem],
        out_specs=vmem,
        scratch_shapes=[
            pltpu.VMEM((n_row, cells, block), BF16),
            pltpu.VMEM((n_space, rows, piece), BF16),
            pltpu.VMEM((cells, block), BF16),
            pltpu.VMEM((2, width_y, block), BF16),
            pltpu.VMEM((groups, sub + 16, slots), BF16),
            pltpu.VMEM((groups, sub + 16, slots), BF16),
            pltpu.VMEM((2, cells, block), F32),
            pltpu.VMEM((2, cells, block), F32),
            pltpu.VMEM((cells, block), BF16),
            pltpu.VMEM((cells, block), BF16),
            dma((hops,)),
            dma((hops,)),
            dma((4,)),
            dma((4,)),
            dma((2,)),
            dma((2,)),
            dma((groups - 1,)),
            dma((groups - 1,)),
            dma((ways,)),
            dma((ways,)),
            dma((2 * CHUNKS,)),
            dma((2 * CHUNKS,)),
            dma((CHUNKS,)),
            dma((CHUNKS,)),
            dma(()),
        ],
        compiler_params=pltpu.CompilerParams(
            collective_id=0, has_side_effects=True, vmem_limit_bytes=60 * 2**20
        ),
        name="iterate",
    )(
        deviation,
        courant,
        collide,
        hole_cells.reshape(1, slots),
        hole_wall.reshape(1, slots),
        specular,
        specularity,
    )
    return result.reshape(width_x, width_y, block)


def solution(mesh):
    sizes = (mesh.shape["space"], mesh.shape["mrow"], mesh.shape["mcol"])
    in_specs = (
        P("space", None, ("mcol", "mrow")),
        P(None, ("mcol", "mrow")),
        P("mrow", ("mcol", "space")),
        P("space"),
        P("space"),
        P(),
        P(),
    )
    out_specs = P("space", None, ("mrow", "mcol"))
    return jax.shard_map(
        functools.partial(on_device, sizes),
        mesh=mesh,
        in_specs=in_specs,
        out_specs=out_specs,
        check_vma=False,
    )
```

```python
import functools

import jax
import jax.numpy as jnp
from jax import lax
from jax.experimental import pallas as pl
from jax.experimental.pallas import tpu as pltpu
from jax.sharding import PartitionSpec as P

MESH = pl.DeviceIdType.MESH
F32 = jnp.float32
BF16 = jnp.bfloat16
PARTS = ((0, 384), (384, 384), (768, 256), (1024, 320), (1344, 192))
CHUNKS = len(PARTS)


def column_of(row, slots):
    return jnp.broadcast_to(row, (128, slots)).T


def widen(tile, count):
    return jnp.concatenate([tile] * count, axis=1)


def body(
    sizes,
    dev_hbm,
    cour_ref,
    coll_hbm,
    cells_ref,
    wall_ref,
    spec_ref,
    share_ref,
    out_hbm,
    out_buf,
    dev_ref,
    cols,
    mats,
    acc,
    read_buf,
    halo,
    msg_out,
    msg_in,
    pair_out,
    pair_in,
    chip_out,
    chip_in,
    z_send,
    z_recv,
    x_send,
    x_recv,
    halo_send,
    halo_recv,
    msg_send,
    msg_recv,
    y_send,
    y_recv,
    pair_send,
    pair_recv,
    chip_send,
    chip_recv,
    own_sem,
    dev_sem,
    out_sem,
):
    n_space, n_row, n_col = sizes
    depth = n_space // 2
    width_x, width_y, block = dev_ref.shape
    cells = width_x * width_y
    slots = cells_ref.shape[0]
    walls, modes = spec_ref.shape
    groups = n_row * n_col
    sub = block // groups
    far = depth // 2
    half = block // 2

    s = lax.axis_index("space")
    y = lax.axis_index("mrow")
    q = lax.axis_index("mcol")
    z, h = s // 2, s % 2
    l, c = q // 2, q % 2
    mate_s = z * 2 + (1 - h)
    z_next = (s + 2) % n_space
    z_prev = (s + n_space - 2) % n_space
    other_s = (s + 2 * h - 1 + n_space) % n_space
    s_next = (s + 1) % n_space
    s_prev = (s + n_space - 1) % n_space
    y_next = (y + 1) % n_row
    y_prev = (y + n_row - 1) % n_row
    core_q = l * 2 + (1 - c)
    chip_q = (1 - l) * 2 + c
    blocks = (
        (1 - l) * 2 + (1 - c),
        (1 - l) * 2 + c,
        l * 2 + (1 - c),
        l * 2 + c,
    )
    mine = q * n_row + y

    peers = []
    for dq in range(n_col):
        for dy in range(n_row):
            if dq or dy:
                peers.append(((y + dy) % n_row, (q + dq) % n_col))

    own_copy = pltpu.make_async_copy(coll_hbm, mats.at[s], own_sem)
    own_copy.start()
    dev_copy = pltpu.make_async_copy(dev_hbm, dev_ref, dev_sem)
    dev_copy.start()
    barrier = pltpu.get_barrier_semaphore()
    for target in (z_next, z_prev, mate_s, other_s):
        pl.semaphore_signal(barrier, inc=1, device_id=(target, y, q), device_id_type=MESH)
    for ty, tq in peers:
        pl.semaphore_signal(barrier, inc=1, device_id=(s, ty, tq), device_id_type=MESH)
    pl.semaphore_wait(barrier, 4 + len(peers))
    own_copy.wait()
    dev_copy.wait()

    started = []

    def remote(src, dst, send, recv, target):
        return pltpu.make_async_remote_copy(
            src_ref=src,
            dst_ref=dst,
            send_sem=send,
            recv_sem=recv,
            device_id=target,
            device_id_type=MESH,
        )

    def go(copy):
        copy.start()
        started.append(copy)

    def rows_of(turn, offset=0, size=None):
        size = block if size is None else size
        return pl.ds(pl.multiple_of(blocks[turn] * block + offset, size), size)

    def cells_of(part):
        start, count = PARTS[part]
        return pl.ds(start, count)

    def z_copy(way, turn, own, hop):
        if way == 0:
            source = (z + depth - (hop - 1)) % depth
            target = z_next
        else:
            source = (z + hop - 1) % depth
            target = z_prev
        slot = source * 2 + (h if own else 1 - h)
        if hop == far:
            rows = rows_of(turn, way * half, half)
        else:
            rows = rows_of(turn)
        index = ((way * 4 + turn) * 2 + own) * far + hop - 1
        ref = mats.at[slot, rows]
        return remote(ref, ref, z_send.at[index], z_recv.at[index], (target, y, q))

    def z_start(turn, own):
        for way in range(2):
            go(z_copy(way, turn, own, 1))

    def z_serve(turn, own, hop):
        for way in range(2):
            z_copy(way, turn, own, hop).wait_recv()
            if hop < far:
                go(z_copy(way, turn, own, hop + 1))
            if own and hop == 1 and turn < 3:
                go(x_copy(turn, 1 + way))

    def z_take(turn):
        for way in range(2):
            z_copy(way, turn, 1, 1).wait_recv()
            go(x_copy(turn, 1 + way))

    def z_pass(turn):
        for way in range(2):
            go(z_copy(way, turn, 1, 2))

    def x_copy(turn, kind):
        source = (z, (z + depth - 1) % depth, (z + 1) % depth)[kind]
        ref = mats.at[source * 2 + h, rows_of(turn)]
        index = turn * 3 + kind
        return remote(ref, ref, x_send.at[index], x_recv.at[index], (mate_s, y, q))

    def x_serve(turn):
        for way in range(2):
            x_copy(turn, 1 + way).wait_recv()
            go(z_copy(way, turn, 0, 2))

    def x_relay(turn):
        x_copy(turn, 0).wait_recv()
        for way in range(2):
            go(z_copy(way, turn, 0, 1))

    def x_finish(turn):
        x_copy(turn, 0).wait_recv()

    def y_copy(way, stage, part):
        target = y_next if way == 0 else y_prev
        if stage == 0:
            owner = y
            rows = cells_of(part)
        else:
            owner = y_prev if way == 0 else y_next
            start, count = PARTS[part]
            rows = pl.ds(start + way * (count // 2), count // 2)
        index = (way * 2 + stage) * CHUNKS + part
        ref = cols.at[owner, rows]
        return remote(ref, ref, y_send.at[index], y_recv.at[index], (s, target, q))

    def y_start(part):
        for way in range(2):
            go(y_copy(way, 0, part))

    def y_forward(part):
        for way in range(2):
            y_copy(way, 0, part).wait_recv()
            go(y_copy(way, 1, part))

    def y_finish(part):
        for way in range(2):
            y_copy(way, 1, part).wait_recv()

    def pair_copy(stage, part):
        rows = cells_of(part)
        index = stage * CHUNKS + part
        return remote(
            pair_out.at[stage, rows],
            pair_in.at[stage, rows],
            pair_send.at[index],
            pair_recv.at[index],
            (s, y, core_q),
        )

    def chip_copy(part):
        rows = cells_of(part)
        return remote(
            chip_out.at[rows],
            chip_in.at[rows],
            chip_send.at[part],
            chip_recv.at[part],
            (s, y, chip_q),
        )

    def product(turn, part):
        rows = cells_of(part)
        total = None
        per = block // mats.shape[2]
        for owner in range(n_row):
            right = jnp.concatenate(
                [mats[owner * per + step, rows_of(turn), :] for step in range(per)], axis=1
            )
            term = lax.dot_general(
                cols[owner, rows, :],
                right,
                (((1,), (1,)), ((), ())),
                preferred_element_type=F32,
            )
            total = term if total is None else total + term
        return total

    halo_up = remote(
        dev_ref.at[width_x - 1], halo.at[0], halo_send.at[0], halo_recv.at[0], (s_next, y, q)
    )
    halo_down = remote(dev_ref.at[0], halo.at[1], halo_send.at[1], halo_recv.at[1], (s_prev, y, q))
    go(halo_up)
    go(halo_down)
    z_start(0, 1)

    reach_x = jnp.abs(cour_ref[0:1, :])
    reach_y = jnp.abs(cour_ref[1:2, :])
    forward_x = cour_ref[0:1, :] > 0
    forward_y = cour_ref[1:2, :] > 0

    def stream(center, before, after):
        mixed = (1.0 - reach_x) * center + reach_x * jnp.where(forward_x, before, after)
        shifted = jnp.where(
            forward_y, pltpu.roll(mixed, 1, 0), pltpu.roll(mixed, width_y - 1, 0)
        )
        return ((1.0 - reach_y) * mixed + reach_y * shifted).astype(BF16)

    def layer(index):
        return dev_ref[index].astype(F32)

    @pl.loop(1, width_x - 1)
    def _(x):
        rows = pl.ds(pl.multiple_of(x * width_y, width_y), width_y)
        read_buf[rows, :] = stream(layer(x), layer(x - 1), layer(x + 1))

    z_start(1, 1)
    halo_up.wait_recv()
    halo_down.wait_recv()
    low = jnp.where(s == 0, 0.0, halo[0].astype(F32))
    high = jnp.where(s == n_space - 1, 0.0, halo[1].astype(F32))
    read_buf[pl.ds(0, width_y), :] = stream(layer(0), low, layer(1))
    read_buf[pl.ds(cells - width_y, width_y), :] = stream(
        layer(width_x - 1), layer(width_x - 2), high
    )

    cells_row = cells_ref[...].reshape(1, slots).astype(F32)
    cells_col = column_of(cells_row, slots)
    lane = lax.broadcasted_iota(jnp.int32, (slots, 128), 1).astype(F32)
    pick = jnp.concatenate(
        [
            jnp.where(cells_col == lane + float(base), 1.0, 0.0).astype(BF16)
            for base in range(0, cells, 128)
        ],
        axis=1,
    )
    rim = jnp.dot(pick, read_buf[...], preferred_element_type=F32).T
    partial = jnp.sum(rim, axis=0, keepdims=True)
    first = partial.astype(BF16).astype(F32)
    second = (partial - first).astype(BF16).astype(F32)
    third = partial - first - second
    line = lax.broadcasted_iota(jnp.int32, (16, slots), 0)
    stats = jnp.where(
        line == 0, first, jnp.where(line == 1, second, jnp.where(line == 2, third, 0.0))
    ).astype(BF16)
    for e in range(groups):
        msg_out[e, 0:sub, :] = rim[e * sub : (e + 1) * sub].astype(BF16)
        msg_out[e, sub : sub + 16, :] = stats
    msg_copies = []
    for index, (ty, tq) in enumerate(peers):
        copy = remote(
            msg_out.at[tq * n_row + ty],
            msg_in.at[mine],
            msg_send.at[index],
            msg_recv.at[index],
            (s, ty, tq),
        )
        go(copy)
        msg_copies.append(copy)
    msg_in[mine] = msg_out[mine]
    z_start(2, 1)
    z_serve(0, 1, 1)
    z_serve(1, 1, 1)

    wall_col = column_of(wall_ref[...].reshape(1, slots).astype(F32), slots)
    table = spec_ref[:, pl.ds(pl.multiple_of(mine * block, block), block)]
    place = (table // block) * sub + table % sub
    share = jnp.zeros((slots, 128), F32)
    for w in range(walls):
        share = jnp.where(wall_col == float(w), share_ref[w], share)

    z_serve(0, 1, 2)
    z_serve(1, 1, 2)
    for copy in msg_copies:
        copy.wait_recv()
    received = msg_in[...].astype(F32)
    inner = received[:, 0:sub, :].reshape(groups * sub, slots).T
    diffuse = jnp.sum(jnp.sum(received[:, sub : sub + 16, :], axis=0), axis=0, keepdims=True)
    diffuse = widen(column_of(diffuse / modes, slots), block // 128)
    spot = lax.broadcasted_iota(jnp.int32, (groups * sub, block), 0)
    mirrored = None
    for w in range(walls):
        chosen = jnp.where(widen(wall_col == float(w), block // 128), inner, 0.0).astype(BF16)
        route = jnp.where(spot == place[w : w + 1, :], 1.0, 0.0).astype(BF16)
        term = jnp.dot(chosen, route, preferred_element_type=F32)
        mirrored = term if mirrored is None else mirrored + term
    share = widen(share, block // 128)
    emitted = (share * mirrored + (1.0 - share) * diffuse).astype(BF16)
    emitted = jnp.concatenate([emitted, jnp.ones((slots, 128), BF16)], axis=1)

    def patch(part):
        start, count = PARTS[part]
        rows = cells_of(part)
        spread = jnp.broadcast_to(cells_row, (count, slots))
        cell_of = lax.broadcasted_iota(jnp.int32, (count, slots), 0).astype(F32)
        place_at = jnp.where(spread == cell_of + float(start), 1.0, 0.0).astype(BF16)
        placed = jnp.dot(place_at, emitted, preferred_element_type=F32)
        hole = widen(placed[:, block:], block // 128) > 0.5
        cols[y, rows, :] = jnp.where(
            hole, placed[:, :block], read_buf[rows, :].astype(F32)
        ).astype(BF16)

    def pass_on(part):
        rows = cells_of(part)
        pair_out[0, rows, :] = product(0, part)
        go(pair_copy(0, part))
        acc[rows, :] = product(1, part)

    def pass_chip(part):
        rows = cells_of(part)
        pair_copy(0, part).wait_recv()
        chip_out[rows, :] = (acc[rows, :] + pair_in[0, rows, :]).astype(BF16)
        go(chip_copy(part))

    patch(0)
    y_start(0)
    patch(1)
    y_start(1)
    for part in range(2, CHUNKS):
        patch(part)

    x_serve(0)
    z_serve(0, 1, 3)
    z_serve(1, 1, 3)
    x_serve(1)
    go(x_copy(0, 0))
    go(x_copy(1, 0))
    z_take(2)
    z_serve(0, 0, 2)
    y_forward(0)
    z_serve(1, 0, 2)
    go(x_copy(3, 0))
    go(x_copy(2, 0))
    z_serve(0, 0, 3)
    y_forward(1)
    y_start(2)
    y_start(3)
    z_serve(1, 0, 3)
    z_pass(2)
    z_start(3, 1)
    x_serve(2)
    x_relay(3)
    for turn in range(2):
        z_serve(turn, 1, 4)
        z_serve(turn, 0, 4)
        x_finish(turn)
    y_finish(0)
    pass_on(0)
    z_serve(2, 1, 2)
    pass_chip(0)
    y_finish(1)
    pass_on(1)
    z_serve(3, 1, 1)
    pass_chip(1)
    z_serve(2, 0, 2)
    y_forward(2)
    z_serve(3, 0, 1)
    z_serve(2, 1, 3)
    y_forward(3)
    y_start(4)
    z_serve(3, 1, 2)
    y_finish(2)
    pass_on(2)
    z_serve(2, 0, 3)
    pass_chip(2)
    z_serve(3, 0, 2)
    y_finish(3)
    pass_on(3)
    pass_chip(3)
    z_serve(3, 1, 3)
    y_forward(4)
    z_serve(2, 1, 4)
    z_serve(2, 0, 4)
    x_finish(2)

    def pass_pair(part):
        pair_out[1, cells_of(part), :] = product(2, part)
        go(pair_copy(1, part))

    pass_pair(0)
    pass_pair(1)
    z_serve(3, 0, 3)
    y_finish(4)
    pass_on(4)
    pass_pair(2)
    pass_chip(4)
    for part in range(3, CHUNKS):
        pass_pair(part)
    z_serve(3, 1, 4)
    z_serve(3, 0, 4)
    out_copies = []
    for part in range(CHUNKS):
        rows = cells_of(part)
        total = product(3, part)
        pair_copy(1, part).wait_recv()
        chip_copy(part).wait_recv()
        out_buf[rows, :] = (
            total + pair_in[1, rows, :] + chip_in[rows, :].astype(F32)
        ).astype(BF16)
        copy = pltpu.make_async_copy(out_buf.at[rows], out_hbm.at[rows], out_sem.at[part])
        copy.start()
        out_copies.append(copy)
    for copy in out_copies:
        copy.wait()
    for copy in started:
        copy.wait_send()


def on_device(sizes, deviation, courant, collide, hole_cells, hole_wall, specular, specularity):
    width_x, width_y, block = deviation.shape
    cells = width_x * width_y
    n_space, n_row, n_col = sizes
    groups = n_row * n_col
    slots = hole_cells.shape[0]
    rows, piece = collide.shape
    vmem = pl.BlockSpec(memory_space=pltpu.VMEM)
    smem = pl.BlockSpec(memory_space=pltpu.SMEM)
    hbm = pl.BlockSpec(memory_space=pl.ANY)
    dma = pltpu.SemaphoreType.DMA
    hops = 2 * 2 * (n_space // 4) * 4
    ways = 2 * 2 * CHUNKS
    sub = block // groups
    result = pl.pallas_call(
        functools.partial(body, sizes),
        out_shape=jax.ShapeDtypeStruct((cells, block), BF16),
        in_specs=[hbm, vmem, hbm, vmem, vmem, vmem, smem],
        out_specs=hbm,
        scratch_shapes=[
            pltpu.VMEM((cells, block), BF16),
            pltpu.VMEM((width_x, width_y, block), BF16),
            pltpu.VMEM((n_row, cells, block), BF16),
            pltpu.VMEM((n_space, rows, piece), BF16),
            pltpu.VMEM((cells, block), F32),
            pltpu.VMEM((cells, block), BF16),
            pltpu.VMEM((2, width_y, block), BF16),
            pltpu.VMEM((groups, sub + 16, slots), BF16),
            pltpu.VMEM((groups, sub + 16, slots), BF16),
            pltpu.VMEM((2, cells, block), F32),
            pltpu.VMEM((2, cells, block), F32),
            pltpu.VMEM((cells, block), BF16),
            pltpu.VMEM((cells, block), BF16),
            dma((hops,)),
            dma((hops,)),
            dma((12,)),
            dma((12,)),
            dma((2,)),
            dma((2,)),
            dma((groups - 1,)),
            dma((groups - 1,)),
            dma((ways,)),
            dma((ways,)),
            dma((2 * CHUNKS,)),
            dma((2 * CHUNKS,)),
            dma((CHUNKS,)),
            dma((CHUNKS,)),
            dma(()),
            dma(()),
            dma((CHUNKS,)),
        ],
        compiler_params=pltpu.CompilerParams(
            collective_id=0, has_side_effects=True, vmem_limit_bytes=60 * 2**20
        ),
        name="iterate",
    )(
        deviation,
        courant,
        collide,
        hole_cells,
        hole_wall,
        specular,
        specularity,
    )
    return result.reshape(width_x, width_y, block)


def solution(mesh):
    sizes = (mesh.shape["space"], mesh.shape["mrow"], mesh.shape["mcol"])
    in_specs = (
        P("space", None, ("mcol", "mrow")),
        P(None, ("mcol", "mrow")),
        P("mrow", ("mcol", "space")),
        P("space"),
        P("space"),
        P(),
        P(),
    )
    out_specs = P("space", None, ("mrow", "mcol"))
    return jax.shard_map(
        functools.partial(on_device, sizes),
        mesh=mesh,
        in_specs=in_specs,
        out_specs=out_specs,
        check_vma=False,
    )
```

```python
import functools

import jax
import jax.numpy as jnp
from jax import lax
from jax.experimental import pallas as pl
from jax.experimental.pallas import tpu as pltpu
from jax.sharding import PartitionSpec as P

MESH = pl.DeviceIdType.MESH
F32 = jnp.float32
BF16 = jnp.bfloat16
PARTS = ((0, 384), (384, 384), (768, 256), (1024, 320), (1344, 192))
CHUNKS = len(PARTS)


def column_of(row, slots):
    return jnp.broadcast_to(row, (128, slots)).T


def widen(tile, count):
    return jnp.concatenate([tile] * count, axis=1)


def body(
    sizes,
    dev_hbm,
    cour_ref,
    coll_hbm,
    cells_ref,
    wall_ref,
    spec_ref,
    share_ref,
    out_hbm,
    out_buf,
    dev_ref,
    cols,
    mats,
    acc,
    read_buf,
    halo,
    msg_out,
    msg_in,
    pair_out,
    pair_in,
    chip_out,
    chip_in,
    z_send,
    z_recv,
    x_send,
    x_recv,
    halo_send,
    halo_recv,
    msg_send,
    msg_recv,
    y_send,
    y_recv,
    pair_send,
    pair_recv,
    chip_send,
    chip_recv,
    own_sem,
    dev_sem,
    out_sem,
):
    n_space, n_row, n_col = sizes
    depth = n_space // 2
    width_x, width_y, block = dev_ref.shape
    cells = width_x * width_y
    slots = cells_ref.shape[0]
    walls, modes = spec_ref.shape
    groups = n_row * n_col
    sub = block // groups
    far = depth // 2
    half = block // 2

    s = lax.axis_index("space")
    y = lax.axis_index("mrow")
    q = lax.axis_index("mcol")
    z, h = s // 2, s % 2
    l, c = q // 2, q % 2
    mate_s = z * 2 + (1 - h)
    z_next = (s + 2) % n_space
    z_prev = (s + n_space - 2) % n_space
    other_s = (s + 2 * h - 1 + n_space) % n_space
    s_next = (s + 1) % n_space
    s_prev = (s + n_space - 1) % n_space
    y_next = (y + 1) % n_row
    y_prev = (y + n_row - 1) % n_row
    core_q = l * 2 + (1 - c)
    chip_q = (1 - l) * 2 + c
    blocks = (
        (1 - l) * 2 + (1 - c),
        (1 - l) * 2 + c,
        l * 2 + (1 - c),
        l * 2 + c,
    )
    mine = q * n_row + y

    peers = []
    for dq in range(n_col):
        for dy in range(n_row):
            if dq or dy:
                peers.append(((y + dy) % n_row, (q + dq) % n_col))

    own_copy = pltpu.make_async_copy(coll_hbm, mats.at[s], own_sem)
    own_copy.start()
    dev_copy = pltpu.make_async_copy(dev_hbm, dev_ref, dev_sem)
    dev_copy.start()
    barrier = pltpu.get_barrier_semaphore()
    for target in (z_next, z_prev, mate_s, other_s):
        pl.semaphore_signal(barrier, inc=1, device_id=(target, y, q), device_id_type=MESH)
    for ty, tq in peers:
        pl.semaphore_signal(barrier, inc=1, device_id=(s, ty, tq), device_id_type=MESH)
    pl.semaphore_wait(barrier, 4 + len(peers))
    own_copy.wait()
    dev_copy.wait()

    started = []

    def remote(src, dst, send, recv, target):
        return pltpu.make_async_remote_copy(
            src_ref=src,
            dst_ref=dst,
            send_sem=send,
            recv_sem=recv,
            device_id=target,
            device_id_type=MESH,
        )

    def go(copy):
        copy.start()
        started.append(copy)

    def rows_of(turn, offset=0, size=None):
        size = block if size is None else size
        return pl.ds(pl.multiple_of(blocks[turn] * block + offset, size), size)

    def cells_of(part):
        start, count = PARTS[part]
        return pl.ds(start, count)

    def z_copy(way, turn, own, hop):
        if way == 0:
            source = (z + depth - (hop - 1)) % depth
            target = z_next
        else:
            source = (z + hop - 1) % depth
            target = z_prev
        slot = source * 2 + (h if own else 1 - h)
        if hop == far:
            rows = rows_of(turn, way * half, half)
        else:
            rows = rows_of(turn)
        index = (turn * 2 + own) * far + hop - 1
        ref = mats.at[slot, rows]
        return remote(ref, ref, z_send.at[turn * 2 + own], z_recv.at[index], (target, y, q))

    def z_both(turn, own, hop):
        index = (turn * 2 + own) * far + hop - 1
        ref = mats.at[0, pl.ds(0, block if hop == far else 2 * block)]
        return remote(ref, ref, z_send.at[turn * 2 + own], z_recv.at[index], (z_next, y, q))

    def z_go(turn, own, hop):
        first = 1 if own or turn == 3 else 2
        if hop > first:
            z_both(turn, own, hop - 1).wait_send()
        for way in range(2):
            z_copy(way, turn, own, hop).start()
        if hop == far:
            started.append(z_both(turn, own, hop))

    def z_start(turn, own):
        z_go(turn, own, 1)

    def z_serve(turn, own, hop):
        z_both(turn, own, hop).wait_recv()
        if hop < far:
            z_go(turn, own, hop + 1)
        if own and hop == 1 and turn < 3:
            x_go(turn)

    def z_take(turn):
        z_both(turn, 1, 1).wait_recv()
        x_go(turn)

    def z_pass(turn):
        z_go(turn, 1, 2)

    def x_copy(turn, kind):
        source = (z, (z + depth - 1) % depth, (z + 1) % depth)[kind]
        ref = mats.at[source * 2 + h, rows_of(turn)]
        index = turn * 2 + min(kind, 1)
        return remote(ref, ref, x_send.at[index], x_recv.at[index], (mate_s, y, q))

    def x_both(turn):
        ref = mats.at[0, pl.ds(0, 2 * block)]
        return remote(
            ref, ref, x_send.at[turn * 2 + 1], x_recv.at[turn * 2 + 1], (mate_s, y, q)
        )

    def x_go(turn):
        for way in range(2):
            x_copy(turn, 1 + way).start()
        started.append(x_both(turn))

    def x_serve(turn):
        x_both(turn).wait_recv()
        z_go(turn, 0, 2)

    def x_relay(turn):
        x_copy(turn, 0).wait_recv()
        z_go(turn, 0, 1)

    def x_finish(turn):
        x_copy(turn, 0).wait_recv()

    def y_copy(way, stage, part):
        target = y_next if way == 0 else y_prev
        if stage == 0:
            owner = y
            rows = cells_of(part)
        else:
            owner = y_prev if way == 0 else y_next
            start, count = PARTS[part]
            rows = pl.ds(start + way * (count // 2), count // 2)
        index = stage * CHUNKS + part
        ref = cols.at[owner, rows]
        return remote(ref, ref, y_send.at[part], y_recv.at[index], (s, target, q))

    def y_both(stage, part):
        count = PARTS[part][1]
        ref = cols.at[0, pl.ds(0, count if stage else 2 * count)]
        return remote(
            ref, ref, y_send.at[part], y_recv.at[stage * CHUNKS + part], (s, y_next, q)
        )

    def y_start(part):
        for way in range(2):
            y_copy(way, 0, part).start()

    def y_forward(part):
        y_both(0, part).wait_recv()
        y_both(0, part).wait_send()
        for way in range(2):
            y_copy(way, 1, part).start()
        started.append(y_both(1, part))

    def y_finish(part):
        y_both(1, part).wait_recv()

    def pair_copy(stage, part):
        rows = cells_of(part)
        index = stage * CHUNKS + part
        return remote(
            pair_out.at[stage, rows],
            pair_in.at[stage, rows],
            pair_send.at[part],
            pair_recv.at[index],
            (s, y, core_q),
        )

    def chip_copy(part):
        rows = cells_of(part)
        return remote(
            chip_out.at[rows],
            chip_in.at[rows],
            chip_send.at[part],
            chip_recv.at[part],
            (s, y, chip_q),
        )

    def product(turn, part):
        rows = cells_of(part)
        total = None
        per = block // mats.shape[2]
        for owner in range(n_row):
            right = jnp.concatenate(
                [mats[owner * per + step, rows_of(turn), :] for step in range(per)], axis=1
            )
            term = lax.dot_general(
                cols[owner, rows, :],
                right,
                (((1,), (1,)), ((), ())),
                preferred_element_type=F32,
            )
            total = term if total is None else total + term
        return total

    def product_of(turn, part, offsets):
        rows = cells_of(part)
        lanes = 2 * mats.shape[2]
        total = None
        for offset in offsets:
            piece = (z + offset + depth) % depth
            owner = piece * lanes // block
            left = cols[owner, rows, pl.ds(pl.multiple_of(piece * lanes % block, lanes), lanes)]
            right = jnp.concatenate(
                [mats[2 * piece, rows_of(turn), :], mats[2 * piece + 1, rows_of(turn), :]], axis=1
            )
            term = lax.dot_general(
                left, right, (((1,), (1,)), ((), ())), preferred_element_type=F32
            )
            total = term if total is None else total + term
        return total

    halo_up = remote(
        dev_ref.at[width_x - 1], halo.at[0], halo_send.at[0], halo_recv.at[0], (s_next, y, q)
    )
    halo_down = remote(dev_ref.at[0], halo.at[1], halo_send.at[1], halo_recv.at[1], (s_prev, y, q))
    go(halo_up)
    go(halo_down)
    z_start(0, 1)

    reach_x = jnp.abs(cour_ref[0:1, :])
    reach_y = jnp.abs(cour_ref[1:2, :])
    forward_x = cour_ref[0:1, :] > 0
    forward_y = cour_ref[1:2, :] > 0

    def stream(center, before, after):
        mixed = (1.0 - reach_x) * center + reach_x * jnp.where(forward_x, before, after)
        shifted = jnp.where(
            forward_y, pltpu.roll(mixed, 1, 0), pltpu.roll(mixed, width_y - 1, 0)
        )
        return ((1.0 - reach_y) * mixed + reach_y * shifted).astype(BF16)

    def layer(index):
        return dev_ref[index].astype(F32)

    @pl.loop(1, width_x - 1)
    def _(x):
        rows = pl.ds(pl.multiple_of(x * width_y, width_y), width_y)
        read_buf[rows, :] = stream(layer(x), layer(x - 1), layer(x + 1))

    z_start(1, 1)
    halo_up.wait_recv()
    halo_down.wait_recv()
    low = jnp.where(s == 0, 0.0, halo[0].astype(F32))
    high = jnp.where(s == n_space - 1, 0.0, halo[1].astype(F32))
    read_buf[pl.ds(0, width_y), :] = stream(layer(0), low, layer(1))
    read_buf[pl.ds(cells - width_y, width_y), :] = stream(
        layer(width_x - 1), layer(width_x - 2), high
    )

    cells_row = cells_ref[...].reshape(1, slots).astype(F32)
    cells_col = column_of(cells_row, slots)
    lane = lax.broadcasted_iota(jnp.int32, (slots, 128), 1).astype(F32)
    pick = jnp.concatenate(
        [
            jnp.where(cells_col == lane + float(base), 1.0, 0.0).astype(BF16)
            for base in range(0, cells, 128)
        ],
        axis=1,
    )
    rim = jnp.dot(pick, read_buf[...], preferred_element_type=F32).T
    partial = jnp.sum(rim, axis=0, keepdims=True)
    first = partial.astype(BF16).astype(F32)
    second = (partial - first).astype(BF16).astype(F32)
    third = partial - first - second
    line = lax.broadcasted_iota(jnp.int32, (16, slots), 0)
    stats = jnp.where(
        line == 0, first, jnp.where(line == 1, second, jnp.where(line == 2, third, 0.0))
    ).astype(BF16)
    for e in range(groups):
        msg_out[e, 0:sub, :] = rim[e * sub : (e + 1) * sub].astype(BF16)
        msg_out[e, sub : sub + 16, :] = stats
    for ty, tq in peers:
        copy = remote(
            msg_out.at[tq * n_row + ty],
            msg_in.at[mine],
            msg_send,
            msg_recv,
            (s, ty, tq),
        )
        copy.start()
    msg_in[mine] = msg_out[mine]
    ref = msg_out.at[pl.ds(0, len(peers))]
    messages = remote(ref, msg_in.at[pl.ds(0, len(peers))], msg_send, msg_recv, (s, y_next, q))
    started.append(messages)
    z_start(2, 1)
    z_serve(0, 1, 1)
    z_serve(1, 1, 1)

    wall_col = column_of(wall_ref[...].reshape(1, slots).astype(F32), slots)
    table = spec_ref[:, pl.ds(pl.multiple_of(mine * block, block), block)]
    place = (table // block) * sub + table % sub
    share = jnp.zeros((slots, 128), F32)
    for w in range(walls):
        share = jnp.where(wall_col == float(w), share_ref[w], share)

    messages.wait_recv()
    received = msg_in[...].astype(F32)
    inner = received[:, 0:sub, :].reshape(groups * sub, slots).T
    diffuse = jnp.sum(jnp.sum(received[:, sub : sub + 16, :], axis=0), axis=0, keepdims=True)
    diffuse = widen(column_of(diffuse / modes, slots), block // 128)
    spot = lax.broadcasted_iota(jnp.int32, (groups * sub, block), 0)
    mirrored = None
    for w in range(walls):
        chosen = jnp.where(widen(wall_col == float(w), block // 128), inner, 0.0).astype(BF16)
        route = jnp.where(spot == place[w : w + 1, :], 1.0, 0.0).astype(BF16)
        term = jnp.dot(chosen, route, preferred_element_type=F32)
        mirrored = term if mirrored is None else mirrored + term
    share = widen(share, block // 128)
    emitted = (share * mirrored + (1.0 - share) * diffuse).astype(BF16)
    emitted = jnp.concatenate([emitted, jnp.ones((slots, 128), BF16)], axis=1)

    def patch(part):
        start, count = PARTS[part]
        rows = cells_of(part)
        spread = jnp.broadcast_to(cells_row, (count, slots))
        cell_of = lax.broadcasted_iota(jnp.int32, (count, slots), 0).astype(F32)
        place_at = jnp.where(spread == cell_of + float(start), 1.0, 0.0).astype(BF16)
        placed = jnp.dot(place_at, emitted, preferred_element_type=F32)
        hole = widen(placed[:, block:], block // 128) > 0.5
        cols[y, rows, :] = jnp.where(
            hole, placed[:, :block], read_buf[rows, :].astype(F32)
        ).astype(BF16)

    def pass_on(part):
        rows = cells_of(part)
        pair_out[0, rows, :] = product(0, part)
        pair_copy(0, part).start()
        acc[rows, :] = product(1, part)

    def pass_chip(part):
        rows = cells_of(part)
        pair_copy(0, part).wait_recv()
        chip_out[rows, :] = (acc[rows, :] + pair_in[0, rows, :]).astype(BF16)
        go(chip_copy(part))

    patch(0)
    y_start(0)
    z_serve(0, 1, 2)
    patch(1)
    y_start(1)
    for part in range(2, CHUNKS):
        patch(part)

    z_serve(1, 1, 2)
    go(x_copy(0, 0))
    go(x_copy(1, 0))
    z_take(2)
    x_serve(0)
    z_serve(0, 1, 3)
    z_serve(1, 1, 3)
    x_serve(1)
    z_serve(0, 0, 2)
    y_forward(0)
    z_serve(1, 0, 2)
    go(x_copy(3, 0))
    go(x_copy(2, 0))
    z_serve(0, 0, 3)
    y_forward(1)
    y_start(2)
    y_start(3)
    z_serve(1, 0, 3)
    z_pass(2)
    z_start(3, 1)
    x_serve(2)
    x_relay(3)
    for turn in range(2):
        z_serve(turn, 1, 4)
        z_serve(turn, 0, 4)
        x_finish(turn)
    y_finish(0)
    pass_on(0)
    z_serve(2, 1, 2)
    pass_chip(0)
    y_finish(1)
    pass_on(1)
    z_serve(3, 1, 1)
    pass_chip(1)
    z_serve(2, 0, 2)
    y_forward(2)
    near = (0, 1, -1)
    mid = near + (2, -2)
    rest = (3, -3, 4)

    def early_pair(part):
        pair_out[1, cells_of(part), :] = product_of(2, part, mid)

    def pass_pair(part):
        rows = cells_of(part)
        if part < 3:
            pair_out[1, rows, :] += product_of(2, part, rest)
        else:
            pair_out[1, rows, :] = product(2, part)
        pair_copy(0, part).wait_send()
        pair_copy(1, part).start()

    def early_own(part, offsets):
        acc[cells_of(part), :] = product_of(3, part, offsets)

    def late_own(part):
        if part < 2:
            return acc[cells_of(part), :] + product_of(3, part, (2, -2) + rest)
        if part == 2:
            return acc[cells_of(part), :] + product_of(3, part, rest)
        return product(3, part)

    x_finish(2)
    early_pair(0)
    early_pair(1)
    z_serve(3, 0, 1)
    early_own(0, near)
    early_own(1, near)
    z_serve(2, 1, 3)
    y_forward(3)
    y_start(4)
    z_serve(3, 1, 2)
    y_finish(2)
    pass_on(2)
    z_serve(2, 0, 3)
    pass_chip(2)
    early_pair(2)
    z_serve(3, 0, 2)
    y_finish(3)
    pass_on(3)
    y_forward(4)
    pass_chip(3)
    early_own(2, mid)
    z_serve(3, 1, 3)
    y_finish(4)
    pass_on(4)
    z_serve(3, 0, 3)
    z_serve(2, 1, 4)
    z_serve(2, 0, 4)
    pass_pair(0)
    pass_chip(4)
    for part in range(1, CHUNKS):
        pass_pair(part)
    z_serve(3, 1, 4)
    z_serve(3, 0, 4)
    for part in range(CHUNKS):
        rows = cells_of(part)
        total = late_own(part)
        pair_copy(1, part).wait_recv()
        chip_copy(part).wait_recv()
        out_buf[rows, :] = (
            total + pair_in[1, rows, :] + chip_in[rows, :].astype(F32)
        ).astype(BF16)
        copy = pltpu.make_async_copy(out_buf.at[rows], out_hbm.at[rows], out_sem)
        copy.start()
    pltpu.make_async_copy(out_buf, out_hbm, out_sem).wait()
    for part in range(CHUNKS):
        pair_copy(1, part).wait_send()
    for copy in started:
        copy.wait_send()


def on_device(sizes, deviation, courant, collide, hole_cells, hole_wall, specular, specularity):
    width_x, width_y, block = deviation.shape
    cells = width_x * width_y
    n_space, n_row, n_col = sizes
    groups = n_row * n_col
    slots = hole_cells.shape[0]
    rows, piece = collide.shape
    vmem = pl.BlockSpec(memory_space=pltpu.VMEM)
    smem = pl.BlockSpec(memory_space=pltpu.SMEM)
    hbm = pl.BlockSpec(memory_space=pl.ANY)
    dma = pltpu.SemaphoreType.DMA
    sub = block // groups
    result = pl.pallas_call(
        functools.partial(body, sizes),
        out_shape=jax.ShapeDtypeStruct((cells, block), BF16),
        in_specs=[hbm, vmem, hbm, vmem, vmem, vmem, smem],
        out_specs=hbm,
        scratch_shapes=[
            pltpu.VMEM((cells, block), BF16),
            pltpu.VMEM((width_x, width_y, block), BF16),
            pltpu.VMEM((n_row, cells, block), BF16),
            pltpu.VMEM((n_space, rows, piece), BF16),
            pltpu.VMEM((cells, block), F32),
            pltpu.VMEM((cells, block), BF16),
            pltpu.VMEM((2, width_y, block), BF16),
            pltpu.VMEM((groups, sub + 16, slots), BF16),
            pltpu.VMEM((groups, sub + 16, slots), BF16),
            pltpu.VMEM((2, cells, block), F32),
            pltpu.VMEM((2, cells, block), F32),
            pltpu.VMEM((cells, block), BF16),
            pltpu.VMEM((cells, block), BF16),
            dma((8,)),
            dma((8 * (n_space // 4),)),
            dma((8,)),
            dma((8,)),
            dma((2,)),
            dma((2,)),
            dma(()),
            dma(()),
            dma((CHUNKS,)),
            dma((2 * CHUNKS,)),
            dma((CHUNKS,)),
            dma((2 * CHUNKS,)),
            dma((CHUNKS,)),
            dma((CHUNKS,)),
            dma(()),
            dma(()),
            dma(()),
        ],
        compiler_params=pltpu.CompilerParams(
            collective_id=0, has_side_effects=True, vmem_limit_bytes=60 * 2**20
        ),
        name="iterate",
    )(
        deviation,
        courant,
        collide,
        hole_cells,
        hole_wall,
        specular,
        specularity,
    )
    return result.reshape(width_x, width_y, block)


def solution(mesh):
    sizes = (mesh.shape["space"], mesh.shape["mrow"], mesh.shape["mcol"])
    in_specs = (
        P("space", None, ("mcol", "mrow")),
        P(None, ("mcol", "mrow")),
        P("mrow", ("mcol", "space")),
        P("space"),
        P("space"),
        P(),
        P(),
    )
    out_specs = P("space", None, ("mrow", "mcol"))
    return jax.shard_map(
        functools.partial(on_device, sizes),
        mesh=mesh,
        in_specs=in_specs,
        out_specs=out_specs,
        check_vma=False,
    )
```

```python
import functools

import jax
import jax.numpy as jnp
from jax import lax
from jax.experimental import pallas as pl
from jax.experimental.pallas import tpu as pltpu
from jax.sharding import PartitionSpec as P

MESH = pl.DeviceIdType.MESH
F32 = jnp.float32
BF16 = jnp.bfloat16
PARTS = ((0, 384), (384, 384), (768, 256), (1024, 320), (1344, 192))
CHUNKS = len(PARTS)


def column_of(row, slots):
    return jnp.broadcast_to(row, (128, slots)).T


def widen(tile, count):
    return jnp.concatenate([tile] * count, axis=1)


def body(
    sizes,
    dev_hbm,
    cour_ref,
    coll_hbm,
    cells_ref,
    wall_ref,
    spec_hbm,
    share_ref,
    out_hbm,
    out_buf,
    spec_ref,
    dev_ref,
    cols,
    mats,
    acc,
    read_buf,
    halo,
    msg_out,
    msg_in,
    pair_out,
    pair_in,
    chip_out,
    chip_in,
    z_send,
    z_recv,
    x_send,
    x_recv,
    halo_send,
    halo_recv,
    msg_send,
    msg_recv,
    y_send,
    y_recv,
    pair_send,
    pair_recv,
    chip_send,
    chip_recv,
    own_sem,
    dev_sem,
    spec_sem,
    out_sem,
):
    n_space, n_row, n_col = sizes
    depth = n_space // 2
    width_x, width_y, block = dev_ref.shape
    cells = width_x * width_y
    slots = cells_ref.shape[0]
    walls, modes = spec_hbm.shape
    groups = n_row * n_col
    sub = block // groups
    far = depth // 2
    half = block // 2

    s = lax.axis_index("space")
    y = lax.axis_index("mrow")
    q = lax.axis_index("mcol")
    z, h = s // 2, s % 2
    l, c = q // 2, q % 2
    mate_s = z * 2 + (1 - h)
    z_next = (s + 2) % n_space
    z_prev = (s + n_space - 2) % n_space
    other_s = (s + 2 * h - 1 + n_space) % n_space
    s_next = (s + 1) % n_space
    s_prev = (s + n_space - 1) % n_space
    y_next = (y + 1) % n_row
    y_prev = (y + n_row - 1) % n_row
    core_q = l * 2 + (1 - c)
    chip_q = (1 - l) * 2 + c
    blocks = (
        (1 - l) * 2 + (1 - c),
        (1 - l) * 2 + c,
        l * 2 + (1 - c),
        l * 2 + c,
    )
    mine = q * n_row + y

    peers = []
    for dq in range(n_col):
        for dy in range(n_row):
            if dq or dy:
                peers.append(((y + dy) % n_row, (q + dq) % n_col))

    own_copy = pltpu.make_async_copy(coll_hbm, mats.at[s], own_sem)
    own_copy.start()
    dev_copy = pltpu.make_async_copy(dev_hbm, dev_ref, dev_sem)
    dev_copy.start()
    columns = pl.ds(pl.multiple_of(mine * block, block), block)
    spec_copy = pltpu.make_async_copy(spec_hbm.at[:, columns], spec_ref, spec_sem)
    spec_copy.start()
    barrier = pltpu.get_barrier_semaphore()
    for target in (z_next, z_prev, mate_s, other_s):
        pl.semaphore_signal(barrier, inc=1, device_id=(target, y, q), device_id_type=MESH)
    for ty, tq in peers:
        pl.semaphore_signal(barrier, inc=1, device_id=(s, ty, tq), device_id_type=MESH)
    pl.semaphore_wait(barrier, 4 + len(peers))
    own_copy.wait()
    dev_copy.wait()
    spec_copy.wait()

    started = []

    def remote(src, dst, send, recv, target):
        return pltpu.make_async_remote_copy(
            src_ref=src,
            dst_ref=dst,
            send_sem=send,
            recv_sem=recv,
            device_id=target,
            device_id_type=MESH,
        )

    def go(copy):
        copy.start()
        started.append(copy)

    def rows_of(turn, offset=0, size=None):
        size = block if size is None else size
        return pl.ds(pl.multiple_of(blocks[turn] * block + offset, size), size)

    def cells_of(part):
        start, count = PARTS[part]
        return pl.ds(start, count)

    def z_copy(way, turn, own, hop):
        if way == 0:
            source = (z + depth - (hop - 1)) % depth
            target = z_next
        else:
            source = (z + hop - 1) % depth
            target = z_prev
        slot = source * 2 + (h if own else 1 - h)
        if hop == far:
            rows = rows_of(turn, way * half, half)
        else:
            rows = rows_of(turn)
        index = (turn * 2 + own) * far + hop - 1
        ref = mats.at[slot, rows]
        return remote(ref, ref, z_send.at[turn * 2 + own], z_recv.at[index], (target, y, q))

    def z_both(turn, own, hop):
        index = (turn * 2 + own) * far + hop - 1
        ref = mats.at[0, pl.ds(0, block if hop == far else 2 * block)]
        return remote(ref, ref, z_send.at[turn * 2 + own], z_recv.at[index], (z_next, y, q))

    def z_go(turn, own, hop):
        first = 1 if own or turn == 3 else 2
        if hop > first:
            z_both(turn, own, hop - 1).wait_send()
        for way in range(2):
            z_copy(way, turn, own, hop).start()
        if hop == far:
            started.append(z_both(turn, own, hop))

    def z_start(turn, own):
        z_go(turn, own, 1)

    def z_serve(turn, own, hop):
        z_both(turn, own, hop).wait_recv()
        if hop < far:
            z_go(turn, own, hop + 1)
        if own and hop == 1 and turn < 3:
            x_go(turn)

    def z_take(turn):
        z_both(turn, 1, 1).wait_recv()
        x_go(turn)

    def z_pass(turn):
        z_go(turn, 1, 2)

    def x_copy(turn, kind):
        source = (z, (z + depth - 1) % depth, (z + 1) % depth)[kind]
        ref = mats.at[source * 2 + h, rows_of(turn)]
        index = turn * 2 + min(kind, 1)
        return remote(ref, ref, x_send.at[index], x_recv.at[index], (mate_s, y, q))

    def x_both(turn):
        ref = mats.at[0, pl.ds(0, 2 * block)]
        return remote(
            ref, ref, x_send.at[turn * 2 + 1], x_recv.at[turn * 2 + 1], (mate_s, y, q)
        )

    def x_go(turn):
        for way in range(2):
            x_copy(turn, 1 + way).start()
        started.append(x_both(turn))

    def x_serve(turn):
        x_both(turn).wait_recv()
        z_go(turn, 0, 2)

    def x_relay(turn):
        x_copy(turn, 0).wait_recv()
        z_go(turn, 0, 1)

    def x_finish(turn):
        x_copy(turn, 0).wait_recv()

    def y_copy(way, stage, part):
        target = y_next if way == 0 else y_prev
        if stage == 0:
            owner = y
            rows = cells_of(part)
        else:
            owner = y_prev if way == 0 else y_next
            start, count = PARTS[part]
            rows = pl.ds(start + way * (count // 2), count // 2)
        index = stage * CHUNKS + part
        ref = cols.at[owner, rows]
        return remote(ref, ref, y_send.at[part], y_recv.at[index], (s, target, q))

    def y_both(stage, part):
        count = PARTS[part][1]
        ref = cols.at[0, pl.ds(0, count if stage else 2 * count)]
        return remote(
            ref, ref, y_send.at[part], y_recv.at[stage * CHUNKS + part], (s, y_next, q)
        )

    def y_start(part):
        for way in range(2):
            y_copy(way, 0, part).start()

    def y_forward(part):
        y_both(0, part).wait_recv()
        y_both(0, part).wait_send()
        for way in range(2):
            y_copy(way, 1, part).start()
        started.append(y_both(1, part))

    def y_finish(part):
        y_both(1, part).wait_recv()

    def pair_copy(stage, part):
        rows = cells_of(part)
        index = stage * CHUNKS + part
        return remote(
            pair_out.at[stage, rows],
            pair_in.at[stage, rows],
            pair_send.at[part],
            pair_recv.at[index],
            (s, y, core_q),
        )

    def chip_copy(part):
        rows = cells_of(part)
        return remote(
            chip_out.at[rows],
            chip_in.at[rows],
            chip_send.at[part],
            chip_recv.at[part],
            (s, y, chip_q),
        )

    def product(turn, part):
        rows = cells_of(part)
        total = None
        per = block // mats.shape[2]
        for owner in range(n_row):
            right = jnp.concatenate(
                [mats[owner * per + step, rows_of(turn), :] for step in range(per)], axis=1
            )
            term = lax.dot_general(
                cols[owner, rows, :],
                right,
                (((1,), (1,)), ((), ())),
                preferred_element_type=F32,
            )
            total = term if total is None else total + term
        return total

    def product_of(turn, part, offsets):
        rows = cells_of(part)
        lanes = 2 * mats.shape[2]
        total = None
        for offset in offsets:
            piece = (z + offset + depth) % depth
            owner = piece * lanes // block
            left = cols[owner, rows, pl.ds(pl.multiple_of(piece * lanes % block, lanes), lanes)]
            right = jnp.concatenate(
                [mats[2 * piece, rows_of(turn), :], mats[2 * piece + 1, rows_of(turn), :]], axis=1
            )
            term = lax.dot_general(
                left, right, (((1,), (1,)), ((), ())), preferred_element_type=F32
            )
            total = term if total is None else total + term
        return total

    halo_up = remote(
        dev_ref.at[width_x - 1], halo.at[0], halo_send.at[0], halo_recv.at[0], (s_next, y, q)
    )
    halo_down = remote(dev_ref.at[0], halo.at[1], halo_send.at[1], halo_recv.at[1], (s_prev, y, q))
    go(halo_up)
    go(halo_down)
    z_start(0, 1)

    reach_x = jnp.abs(cour_ref[0:1, :])
    reach_y = jnp.abs(cour_ref[1:2, :])
    forward_x = cour_ref[0:1, :] > 0
    forward_y = cour_ref[1:2, :] > 0

    def stream(center, before, after):
        mixed = (1.0 - reach_x) * center + reach_x * jnp.where(forward_x, before, after)
        shifted = jnp.where(
            forward_y, pltpu.roll(mixed, 1, 0), pltpu.roll(mixed, width_y - 1, 0)
        )
        return ((1.0 - reach_y) * mixed + reach_y * shifted).astype(BF16)

    def layer(index):
        return dev_ref[index].astype(F32)

    @pl.loop(1, width_x - 1)
    def _(x):
        rows = pl.ds(pl.multiple_of(x * width_y, width_y), width_y)
        read_buf[rows, :] = stream(layer(x), layer(x - 1), layer(x + 1))

    z_start(1, 1)
    halo_up.wait_recv()
    halo_down.wait_recv()
    low = jnp.where(s == 0, 0.0, halo[0].astype(F32))
    high = jnp.where(s == n_space - 1, 0.0, halo[1].astype(F32))
    read_buf[pl.ds(0, width_y), :] = stream(layer(0), low, layer(1))
    read_buf[pl.ds(cells - width_y, width_y), :] = stream(
        layer(width_x - 1), layer(width_x - 2), high
    )

    cells_row = cells_ref[...].reshape(1, slots).astype(F32)
    cells_col = column_of(cells_row, slots)
    lane = lax.broadcasted_iota(jnp.int32, (slots, 128), 1).astype(F32)
    pick = jnp.concatenate(
        [
            jnp.where(cells_col == lane + float(base), 1.0, 0.0).astype(BF16)
            for base in range(0, cells, 128)
        ],
        axis=1,
    )
    rim = jnp.dot(pick, read_buf[...], preferred_element_type=F32).T
    partial = jnp.sum(rim, axis=0, keepdims=True)
    first = partial.astype(BF16).astype(F32)
    second = (partial - first).astype(BF16).astype(F32)
    third = partial - first - second
    line = lax.broadcasted_iota(jnp.int32, (16, slots), 0)
    stats = jnp.where(
        line == 0, first, jnp.where(line == 1, second, jnp.where(line == 2, third, 0.0))
    ).astype(BF16)
    for e in range(groups):
        msg_out[e, 0:sub, :] = rim[e * sub : (e + 1) * sub].astype(BF16)
        msg_out[e, sub : sub + 16, :] = stats
    for ty, tq in peers:
        copy = remote(
            msg_out.at[tq * n_row + ty],
            msg_in.at[mine],
            msg_send,
            msg_recv,
            (s, ty, tq),
        )
        copy.start()
    msg_in[mine] = msg_out[mine]
    ref = msg_out.at[pl.ds(0, len(peers))]
    messages = remote(ref, msg_in.at[pl.ds(0, len(peers))], msg_send, msg_recv, (s, y_next, q))
    started.append(messages)
    z_start(2, 1)
    z_serve(0, 1, 1)
    z_serve(1, 1, 1)

    wall_col = column_of(wall_ref[...].reshape(1, slots).astype(F32), slots)
    table = spec_ref[...]
    place = (table // block) * sub + table % sub
    share = jnp.zeros((slots, 128), F32)
    for w in range(walls):
        share = jnp.where(wall_col == float(w), share_ref[w], share)

    messages.wait_recv()
    received = msg_in[...].astype(F32)
    inner = received[:, 0:sub, :].reshape(groups * sub, slots).T
    diffuse = jnp.sum(jnp.sum(received[:, sub : sub + 16, :], axis=0), axis=0, keepdims=True)
    diffuse = widen(column_of(diffuse / modes, slots), block // 128)
    spot = lax.broadcasted_iota(jnp.int32, (groups * sub, block), 0)
    mirrored = None
    for w in range(walls):
        chosen = jnp.where(widen(wall_col == float(w), block // 128), inner, 0.0).astype(BF16)
        route = jnp.where(spot == place[w : w + 1, :], 1.0, 0.0).astype(BF16)
        term = jnp.dot(chosen, route, preferred_element_type=F32)
        mirrored = term if mirrored is None else mirrored + term
    share = widen(share, block // 128)
    emitted = (share * mirrored + (1.0 - share) * diffuse).astype(BF16)
    emitted = jnp.concatenate([emitted, jnp.ones((slots, 128), BF16)], axis=1)

    def patch(part):
        start, count = PARTS[part]
        rows = cells_of(part)
        spread = jnp.broadcast_to(cells_row, (count, slots))
        cell_of = lax.broadcasted_iota(jnp.int32, (count, slots), 0).astype(F32)
        place_at = jnp.where(spread == cell_of + float(start), 1.0, 0.0).astype(BF16)
        placed = jnp.dot(place_at, emitted, preferred_element_type=F32)
        hole = widen(placed[:, block:], block // 128) > 0.5
        cols[y, rows, :] = jnp.where(
            hole, placed[:, :block], read_buf[rows, :].astype(F32)
        ).astype(BF16)

    def pass_first(part):
        pair_out[0, cells_of(part), :] = product(0, part)
        pair_copy(0, part).start()

    def pass_second(part):
        acc[cells_of(part), :] = product(1, part)

    def pass_on(part):
        pass_first(part)
        pass_second(part)

    def pass_chip(part):
        rows = cells_of(part)
        pair_copy(0, part).wait_recv()
        chip_out[rows, :] = (acc[rows, :] + pair_in[0, rows, :]).astype(BF16)
        go(chip_copy(part))

    patch(0)
    y_start(0)
    z_serve(0, 1, 2)
    patch(1)
    y_start(1)
    for part in range(2, CHUNKS):
        patch(part)

    z_serve(1, 1, 2)
    go(x_copy(0, 0))
    go(x_copy(1, 0))
    z_take(2)
    x_serve(0)
    z_serve(0, 1, 3)
    z_serve(1, 1, 3)
    x_serve(1)
    z_serve(0, 0, 2)
    y_forward(0)
    z_serve(1, 0, 2)
    go(x_copy(3, 0))
    go(x_copy(2, 0))
    z_serve(0, 0, 3)
    y_forward(1)
    y_start(2)
    y_start(3)
    z_serve(1, 0, 3)
    z_pass(2)
    z_start(3, 1)
    x_serve(2)
    x_relay(3)
    z_serve(0, 1, 4)
    z_serve(0, 0, 4)
    x_finish(0)
    y_finish(0)
    pass_first(0)
    z_serve(1, 1, 4)
    z_serve(1, 0, 4)
    x_finish(1)
    pass_second(0)
    pass_chip(0)
    z_serve(2, 1, 2)
    y_finish(1)
    pass_on(1)
    z_serve(3, 1, 1)
    pass_chip(1)
    z_serve(2, 0, 2)
    y_forward(2)
    near = (0, 1, -1)
    mid = near + (2, -2)
    rest = (3, -3, 4)

    def early_pair(part):
        pair_out[1, cells_of(part), :] = product_of(2, part, mid)

    def pass_pair(part):
        rows = cells_of(part)
        if part < 3:
            pair_out[1, rows, :] += product_of(2, part, rest)
        else:
            pair_out[1, rows, :] = product(2, part)
        pair_copy(0, part).wait_send()
        pair_copy(1, part).start()

    def early_own(part, offsets):
        acc[cells_of(part), :] = product_of(3, part, offsets)

    def more_own(part):
        acc[cells_of(part), :] += product_of(3, part, (2, -2))

    def late_own(part):
        if part < 4:
            return acc[cells_of(part), :] + product_of(3, part, rest)
        return product(3, part)

    x_finish(2)
    early_pair(0)
    early_pair(1)
    z_serve(3, 0, 1)
    early_own(0, near)
    early_own(1, near)
    z_serve(2, 1, 3)
    y_forward(3)
    y_start(4)
    z_serve(3, 1, 2)
    y_finish(2)
    pass_on(2)
    z_serve(2, 0, 3)
    pass_chip(2)
    early_pair(2)
    z_serve(3, 0, 2)
    y_finish(3)
    pass_on(3)
    y_forward(4)
    pass_chip(3)
    early_own(2, mid)
    early_own(3, mid)
    more_own(0)
    more_own(1)
    z_serve(3, 1, 3)
    z_serve(2, 1, 4)
    z_serve(2, 0, 4)
    pass_pair(0)
    y_finish(4)
    pass_first(4)
    z_serve(3, 0, 3)
    pass_second(4)
    pass_chip(4)
    for part in range(1, CHUNKS):
        pass_pair(part)
    z_serve(3, 1, 4)
    z_serve(3, 0, 4)
    for part in range(CHUNKS):
        rows = cells_of(part)
        total = late_own(part)
        pair_copy(1, part).wait_recv()
        chip_copy(part).wait_recv()
        out_buf[rows, :] = (
            total + pair_in[1, rows, :] + chip_in[rows, :].astype(F32)
        ).astype(BF16)
        copy = pltpu.make_async_copy(out_buf.at[rows], out_hbm.at[rows], out_sem)
        copy.start()
    pltpu.make_async_copy(out_buf, out_hbm, out_sem).wait()
    for part in range(CHUNKS):
        pair_copy(1, part).wait_send()
    for copy in started:
        copy.wait_send()


def on_device(sizes, deviation, courant, collide, hole_cells, hole_wall, specular, specularity):
    width_x, width_y, block = deviation.shape
    cells = width_x * width_y
    n_space, n_row, n_col = sizes
    groups = n_row * n_col
    slots = hole_cells.shape[0]
    rows, piece = collide.shape
    vmem = pl.BlockSpec(memory_space=pltpu.VMEM)
    smem = pl.BlockSpec(memory_space=pltpu.SMEM)
    hbm = pl.BlockSpec(memory_space=pl.ANY)
    dma = pltpu.SemaphoreType.DMA
    sub = block // groups
    result = pl.pallas_call(
        functools.partial(body, sizes),
        out_shape=jax.ShapeDtypeStruct((cells, block), BF16),
        in_specs=[hbm, vmem, hbm, vmem, vmem, hbm, smem],
        out_specs=hbm,
        scratch_shapes=[
            pltpu.VMEM((cells, block), BF16),
            pltpu.VMEM((specular.shape[0], block), jnp.int32),
            pltpu.VMEM((width_x, width_y, block), BF16),
            pltpu.VMEM((n_row, cells, block), BF16),
            pltpu.VMEM((n_space, rows, piece), BF16),
            pltpu.VMEM((cells, block), F32),
            pltpu.VMEM((cells, block), BF16),
            pltpu.VMEM((2, width_y, block), BF16),
            pltpu.VMEM((groups, sub + 16, slots), BF16),
            pltpu.VMEM((groups, sub + 16, slots), BF16),
            pltpu.VMEM((2, cells, block), F32),
            pltpu.VMEM((2, cells, block), F32),
            pltpu.VMEM((cells, block), BF16),
            pltpu.VMEM((cells, block), BF16),
            dma((8,)),
            dma((8 * (n_space // 4),)),
            dma((8,)),
            dma((8,)),
            dma((2,)),
            dma((2,)),
            dma(()),
            dma(()),
            dma((CHUNKS,)),
            dma((2 * CHUNKS,)),
            dma((CHUNKS,)),
            dma((2 * CHUNKS,)),
            dma((CHUNKS,)),
            dma((CHUNKS,)),
            dma(()),
            dma(()),
            dma(()),
            dma(()),
        ],
        compiler_params=pltpu.CompilerParams(
            collective_id=0, has_side_effects=True, vmem_limit_bytes=60 * 2**20
        ),
        name="iterate",
    )(
        deviation,
        courant,
        collide,
        hole_cells,
        hole_wall,
        specular,
        specularity,
    )
    return result.reshape(width_x, width_y, block)


def solution(mesh):
    sizes = (mesh.shape["space"], mesh.shape["mrow"], mesh.shape["mcol"])
    in_specs = (
        P("space", None, ("mcol", "mrow")),
        P(None, ("mcol", "mrow")),
        P("mrow", ("mcol", "space")),
        P("space"),
        P("space"),
        P(),
        P(),
    )
    out_specs = P("space", None, ("mrow", "mcol"))
    return jax.shard_map(
        functools.partial(on_device, sizes),
        mesh=mesh,
        in_specs=in_specs,
        out_specs=out_specs,
        check_vma=False,
    )
```

```python
import functools

import jax
import jax.numpy as jnp
from jax import lax
from jax.experimental import pallas as pl
from jax.experimental.pallas import tpu as pltpu
from jax.sharding import PartitionSpec as P

MESH = pl.DeviceIdType.MESH
F32 = jnp.float32
BF16 = jnp.bfloat16
PARTS = ((0, 384), (384, 384), (768, 256), (1024, 320), (1344, 192))
CHUNKS = len(PARTS)


def column_of(row, slots):
    return jnp.broadcast_to(row, (128, slots)).T


def widen(tile, count):
    return jnp.concatenate([tile] * count, axis=1)


def body(
    sizes,
    dev_hbm,
    cour_ref,
    coll_hbm,
    cells_ref,
    wall_ref,
    spec_hbm,
    share_ref,
    out_hbm,
    out_buf,
    spec_ref,
    dev_ref,
    cols,
    mats,
    acc,
    read_buf,
    halo,
    msg_out,
    msg_in,
    pair_out,
    pair_in,
    chip_out,
    chip_in,
    z_send,
    z_recv,
    x_send,
    x_recv,
    halo_send,
    halo_recv,
    msg_send,
    msg_recv,
    y_send,
    y_recv,
    pair_send,
    pair_recv,
    chip_send,
    chip_recv,
    own_sem,
    dev_sem,
    spec_sem,
    out_sem,
):
    n_space, n_row, n_col = sizes
    depth = n_space // 2
    width_x, width_y, block = dev_ref.shape
    cells = width_x * width_y
    slots = cells_ref.shape[0]
    walls, modes = spec_hbm.shape
    groups = n_row * n_col
    sub = block // groups
    far = depth // 2
    half = block // 2

    s = lax.axis_index("space")
    y = lax.axis_index("mrow")
    q = lax.axis_index("mcol")
    z, h = s // 2, s % 2
    l, c = q // 2, q % 2
    mate_s = z * 2 + (1 - h)
    z_next = (s + 2) % n_space
    z_prev = (s + n_space - 2) % n_space
    other_s = (s + 2 * h - 1 + n_space) % n_space
    s_next = (s + 1) % n_space
    s_prev = (s + n_space - 1) % n_space
    y_next = (y + 1) % n_row
    y_prev = (y + n_row - 1) % n_row
    core_q = l * 2 + (1 - c)
    chip_q = (1 - l) * 2 + c
    blocks = (
        (1 - l) * 2 + (1 - c),
        (1 - l) * 2 + c,
        l * 2 + (1 - c),
        l * 2 + c,
    )
    mine = q * n_row + y

    peers = []
    for dq in range(n_col):
        for dy in range(n_row):
            if dq or dy:
                peers.append(((y + dy) % n_row, (q + dq) % n_col))

    own_copy = pltpu.make_async_copy(coll_hbm, mats.at[s], own_sem)
    own_copy.start()
    dev_copy = pltpu.make_async_copy(dev_hbm, dev_ref, dev_sem)
    dev_copy.start()
    columns = pl.ds(pl.multiple_of(mine * block, block), block)
    spec_copy = pltpu.make_async_copy(spec_hbm.at[:, columns], spec_ref, spec_sem)
    spec_copy.start()
    barrier = pltpu.get_barrier_semaphore()
    for target in (z_next, z_prev, mate_s, other_s):
        pl.semaphore_signal(barrier, inc=1, device_id=(target, y, q), device_id_type=MESH)
    for ty, tq in peers:
        pl.semaphore_signal(barrier, inc=1, device_id=(s, ty, tq), device_id_type=MESH)
    pl.semaphore_wait(barrier, 4 + len(peers))
    own_copy.wait()
    dev_copy.wait()
    spec_copy.wait()

    started = []

    def remote(src, dst, send, recv, target):
        return pltpu.make_async_remote_copy(
            src_ref=src,
            dst_ref=dst,
            send_sem=send,
            recv_sem=recv,
            device_id=target,
            device_id_type=MESH,
        )

    def go(copy):
        copy.start()
        started.append(copy)

    def rows_of(turn, offset=0, size=None):
        size = block if size is None else size
        return pl.ds(pl.multiple_of(blocks[turn] * block + offset, size), size)

    def cells_of(part):
        start, count = PARTS[part]
        return pl.ds(start, count)

    def z_copy(way, turn, own, hop):
        if way == 0:
            source = (z + depth - (hop - 1)) % depth
            target = z_next
        else:
            source = (z + hop - 1) % depth
            target = z_prev
        slot = source * 2 + (h if own else 1 - h)
        if hop == far:
            rows = rows_of(turn, way * half, half)
        else:
            rows = rows_of(turn)
        index = (turn * 2 + own) * far + hop - 1
        ref = mats.at[slot, rows]
        return remote(ref, ref, z_send.at[turn * 2 + own], z_recv.at[index], (target, y, q))

    def z_both(turn, own, hop):
        index = (turn * 2 + own) * far + hop - 1
        ref = mats.at[0, pl.ds(0, block if hop == far else 2 * block)]
        return remote(ref, ref, z_send.at[turn * 2 + own], z_recv.at[index], (z_next, y, q))

    def z_go(turn, own, hop):
        first = 1 if own or turn == 3 else 2
        if hop > first:
            z_both(turn, own, hop - 1).wait_send()
        for way in range(2):
            z_copy(way, turn, own, hop).start()
        if hop == far:
            started.append(z_both(turn, own, hop))

    def z_start(turn, own):
        z_go(turn, own, 1)

    def z_serve(turn, own, hop):
        z_both(turn, own, hop).wait_recv()
        if hop < far:
            z_go(turn, own, hop + 1)
        if own and hop == 1 and turn < 3:
            x_go(turn)

    def z_take(turn):
        z_both(turn, 1, 1).wait_recv()
        x_go(turn)

    def z_pass(turn):
        z_go(turn, 1, 2)

    def x_copy(turn, kind):
        source = (z, (z + depth - 1) % depth, (z + 1) % depth)[kind]
        ref = mats.at[source * 2 + h, rows_of(turn)]
        index = turn * 2 + min(kind, 1)
        return remote(ref, ref, x_send.at[index], x_recv.at[index], (mate_s, y, q))

    def x_both(turn):
        ref = mats.at[0, pl.ds(0, 2 * block)]
        return remote(
            ref, ref, x_send.at[turn * 2 + 1], x_recv.at[turn * 2 + 1], (mate_s, y, q)
        )

    def x_go(turn):
        for way in range(2):
            x_copy(turn, 1 + way).start()
        started.append(x_both(turn))

    def x_serve(turn):
        x_both(turn).wait_recv()
        z_go(turn, 0, 2)

    def x_relay(turn):
        x_copy(turn, 0).wait_recv()
        z_go(turn, 0, 1)

    def x_finish(turn):
        x_copy(turn, 0).wait_recv()

    def y_copy(way, stage, part):
        target = y_next if way == 0 else y_prev
        if stage == 0:
            owner = y
            rows = cells_of(part)
        else:
            owner = y_prev if way == 0 else y_next
            start, count = PARTS[part]
            rows = pl.ds(start + way * (count // 2), count // 2)
        index = stage * CHUNKS + part
        ref = cols.at[owner, rows]
        return remote(ref, ref, y_send.at[part], y_recv.at[index], (s, target, q))

    def y_both(stage, part):
        count = PARTS[part][1]
        ref = cols.at[0, pl.ds(0, count if stage else 2 * count)]
        return remote(
            ref, ref, y_send.at[part], y_recv.at[stage * CHUNKS + part], (s, y_next, q)
        )

    def y_start(part):
        for way in range(2):
            y_copy(way, 0, part).start()

    def y_forward(part):
        y_both(0, part).wait_recv()
        y_both(0, part).wait_send()
        for way in range(2):
            y_copy(way, 1, part).start()
        started.append(y_both(1, part))

    def y_finish(part):
        y_both(1, part).wait_recv()

    def pair_copy(stage, part):
        rows = cells_of(part)
        index = stage * CHUNKS + part
        return remote(
            pair_out.at[stage, rows],
            pair_in.at[stage, rows],
            pair_send.at[part],
            pair_recv.at[index],
            (s, y, core_q),
        )

    def chip_copy(part):
        rows = cells_of(part)
        return remote(
            chip_out.at[rows],
            chip_in.at[rows],
            chip_send.at[part],
            chip_recv.at[part],
            (s, y, chip_q),
        )

    def product(turn, part):
        rows = cells_of(part)
        total = None
        per = block // mats.shape[2]
        for owner in range(n_row):
            right = jnp.concatenate(
                [mats[owner * per + step, rows_of(turn), :] for step in range(per)], axis=1
            )
            term = lax.dot_general(
                cols[owner, rows, :],
                right,
                (((1,), (1,)), ((), ())),
                preferred_element_type=F32,
            )
            total = term if total is None else total + term
        return total

    def product_of(turn, part, offsets):
        rows = cells_of(part)
        lanes = 2 * mats.shape[2]
        total = None
        for offset in offsets:
            piece = (z + offset + depth) % depth
            owner = piece * lanes // block
            left = cols[owner, rows, pl.ds(pl.multiple_of(piece * lanes % block, lanes), lanes)]
            right = jnp.concatenate(
                [mats[2 * piece, rows_of(turn), :], mats[2 * piece + 1, rows_of(turn), :]], axis=1
            )
            term = lax.dot_general(
                left, right, (((1,), (1,)), ((), ())), preferred_element_type=F32
            )
            total = term if total is None else total + term
        return total

    halo_up = remote(
        dev_ref.at[width_x - 1], halo.at[0], halo_send.at[0], halo_recv.at[0], (s_next, y, q)
    )
    halo_down = remote(dev_ref.at[0], halo.at[1], halo_send.at[1], halo_recv.at[1], (s_prev, y, q))
    go(halo_up)
    go(halo_down)
    z_start(0, 1)

    reach_x = jnp.abs(cour_ref[0:1, :])
    reach_y = jnp.abs(cour_ref[1:2, :])
    forward_x = cour_ref[0:1, :] > 0
    forward_y = cour_ref[1:2, :] > 0

    def stream(center, before, after):
        mixed = (1.0 - reach_x) * center + reach_x * jnp.where(forward_x, before, after)
        shifted = jnp.where(
            forward_y, pltpu.roll(mixed, 1, 0), pltpu.roll(mixed, width_y - 1, 0)
        )
        return ((1.0 - reach_y) * mixed + reach_y * shifted).astype(BF16)

    def layer(index):
        return dev_ref[index].astype(F32)

    @pl.loop(1, width_x - 1)
    def _(x):
        rows = pl.ds(pl.multiple_of(x * width_y, width_y), width_y)
        read_buf[rows, :] = stream(layer(x), layer(x - 1), layer(x + 1))

    z_start(1, 1)
    halo_up.wait_recv()
    halo_down.wait_recv()
    low = jnp.where(s == 0, 0.0, halo[0].astype(F32))
    high = jnp.where(s == n_space - 1, 0.0, halo[1].astype(F32))
    read_buf[pl.ds(0, width_y), :] = stream(layer(0), low, layer(1))
    read_buf[pl.ds(cells - width_y, width_y), :] = stream(
        layer(width_x - 1), layer(width_x - 2), high
    )

    cells_row = cells_ref[...].reshape(1, slots).astype(F32)
    cells_col = column_of(cells_row, slots)
    lane = lax.broadcasted_iota(jnp.int32, (slots, 128), 1).astype(F32)
    pick = jnp.concatenate(
        [
            jnp.where(cells_col == lane + float(base), 1.0, 0.0).astype(BF16)
            for base in range(0, cells, 128)
        ],
        axis=1,
    )
    rim = jnp.dot(pick, read_buf[...], preferred_element_type=F32).T
    partial = jnp.sum(rim, axis=0, keepdims=True)
    first = partial.astype(BF16).astype(F32)
    second = (partial - first).astype(BF16).astype(F32)
    third = partial - first - second
    line = lax.broadcasted_iota(jnp.int32, (16, slots), 0)
    stats = jnp.where(
        line == 0, first, jnp.where(line == 1, second, jnp.where(line == 2, third, 0.0))
    ).astype(BF16)
    for e in range(groups):
        msg_out[e, 0:sub, :] = rim[e * sub : (e + 1) * sub].astype(BF16)
        msg_out[e, sub : sub + 16, :] = stats
    for ty, tq in peers:
        copy = remote(
            msg_out.at[tq * n_row + ty],
            msg_in.at[mine],
            msg_send,
            msg_recv,
            (s, ty, tq),
        )
        copy.start()
    msg_in[mine] = msg_out[mine]
    ref = msg_out.at[pl.ds(0, len(peers))]
    messages = remote(ref, msg_in.at[pl.ds(0, len(peers))], msg_send, msg_recv, (s, y_next, q))
    started.append(messages)
    z_start(2, 1)
    z_serve(0, 1, 1)
    z_serve(1, 1, 1)

    wall_col = column_of(wall_ref[...].reshape(1, slots).astype(F32), slots)
    table = spec_ref[...]
    place = (table // block) * sub + table % sub
    share = jnp.zeros((slots, 128), F32)
    for w in range(walls):
        share = jnp.where(wall_col == float(w), share_ref[w], share)

    messages.wait_recv()
    received = msg_in[...].astype(F32)
    inner = received[:, 0:sub, :].reshape(groups * sub, slots).T
    diffuse = jnp.sum(jnp.sum(received[:, sub : sub + 16, :], axis=0), axis=0, keepdims=True)
    diffuse = widen(column_of(diffuse / modes, slots), block // 128)
    spot = lax.broadcasted_iota(jnp.int32, (groups * sub, block), 0)
    mirrored = None
    for w in range(walls):
        chosen = jnp.where(widen(wall_col == float(w), block // 128), inner, 0.0).astype(BF16)
        route = jnp.where(spot == place[w : w + 1, :], 1.0, 0.0).astype(BF16)
        term = jnp.dot(chosen, route, preferred_element_type=F32)
        mirrored = term if mirrored is None else mirrored + term
    share = widen(share, block // 128)
    emitted = (share * mirrored + (1.0 - share) * diffuse).astype(BF16)
    emitted = jnp.concatenate([emitted, jnp.ones((slots, 128), BF16)], axis=1)

    def patch(part):
        start, count = PARTS[part]
        rows = cells_of(part)
        spread = jnp.broadcast_to(cells_row, (count, slots))
        cell_of = lax.broadcasted_iota(jnp.int32, (count, slots), 0).astype(F32)
        place_at = jnp.where(spread == cell_of + float(start), 1.0, 0.0).astype(BF16)
        placed = jnp.dot(place_at, emitted, preferred_element_type=F32)
        hole = widen(placed[:, block:], block // 128) > 0.5
        cols[y, rows, :] = jnp.where(
            hole, placed[:, :block], read_buf[rows, :].astype(F32)
        ).astype(BF16)

    def pass_first(part):
        pair_out[0, cells_of(part), :] = product(0, part)
        pair_copy(0, part).start()

    def pass_second(part):
        acc[cells_of(part), :] = product(1, part)

    def pass_on(part):
        pass_first(part)
        pass_second(part)

    def pass_chip(part):
        rows = cells_of(part)
        pair_copy(0, part).wait_recv()
        chip_out[rows, :] = (acc[rows, :] + pair_in[0, rows, :]).astype(BF16)
        go(chip_copy(part))

    patch(0)
    y_start(0)
    z_serve(0, 1, 2)
    patch(1)
    y_start(1)
    for part in range(2, CHUNKS):
        patch(part)

    z_serve(1, 1, 2)
    go(x_copy(0, 0))
    go(x_copy(1, 0))
    z_take(2)
    x_serve(0)
    z_serve(0, 1, 3)
    z_serve(1, 1, 3)
    x_serve(1)
    z_serve(0, 0, 2)
    y_forward(0)
    z_serve(1, 0, 2)
    go(x_copy(3, 0))
    go(x_copy(2, 0))
    z_serve(0, 0, 3)
    y_forward(1)
    y_start(2)
    y_start(3)
    z_serve(1, 0, 3)
    z_pass(2)
    z_start(3, 1)
    x_serve(2)
    x_relay(3)
    z_serve(0, 1, 4)
    z_serve(0, 0, 4)
    x_finish(0)
    y_finish(0)
    pass_first(0)
    z_serve(1, 1, 4)
    z_serve(1, 0, 4)
    x_finish(1)
    pass_second(0)
    pass_chip(0)
    z_serve(2, 1, 2)
    y_finish(1)
    pass_on(1)
    z_serve(3, 1, 1)
    pass_chip(1)
    z_serve(2, 0, 2)
    y_forward(2)
    near = (0, 1, -1)
    mid = near + (2, -2)
    rest = (3, -3, 4)

    def early_pair(part):
        pair_out[1, cells_of(part), :] = product_of(2, part, mid)

    def pass_pair(part):
        rows = cells_of(part)
        if part < 3:
            pair_out[1, rows, :] += product_of(2, part, rest)
        else:
            pair_out[1, rows, :] = product(2, part)
        pair_copy(0, part).wait_send()
        pair_copy(1, part).start()

    def early_own(part, offsets):
        acc[cells_of(part), :] = product_of(3, part, offsets)

    def more_own(part):
        acc[cells_of(part), :] += product_of(3, part, (2, -2))

    def late_own(part):
        if part < 4:
            return acc[cells_of(part), :] + product_of(3, part, rest)
        return product(3, part)

    x_finish(2)
    early_pair(0)
    early_pair(1)
    z_serve(3, 0, 1)
    early_own(0, near)
    early_own(1, near)
    z_serve(2, 1, 3)
    y_forward(3)
    y_start(4)
    z_serve(3, 1, 2)
    y_finish(2)
    pass_on(2)
    z_serve(2, 0, 3)
    pass_chip(2)
    early_pair(2)
    z_serve(3, 0, 2)
    y_finish(3)
    pass_on(3)
    y_forward(4)
    early_own(2, mid)
    more_own(0)
    pass_chip(3)
    early_own(3, mid)
    more_own(1)
    z_serve(3, 1, 3)
    z_serve(2, 1, 4)
    z_serve(2, 0, 4)
    pass_pair(0)
    y_finish(4)
    pass_first(4)
    z_serve(3, 0, 3)
    pass_second(4)
    pass_pair(1)
    pass_chip(4)
    for part in range(2, CHUNKS):
        pass_pair(part)
    z_serve(3, 1, 4)
    z_serve(3, 0, 4)
    for part in range(CHUNKS):
        rows = cells_of(part)
        total = late_own(part)
        pair_copy(1, part).wait_recv()
        chip_copy(part).wait_recv()
        out_buf[rows, :] = (
            total + pair_in[1, rows, :] + chip_in[rows, :].astype(F32)
        ).astype(BF16)
        copy = pltpu.make_async_copy(out_buf.at[rows], out_hbm.at[rows], out_sem)
        copy.start()
    pltpu.make_async_copy(out_buf, out_hbm, out_sem).wait()
    for part in range(CHUNKS):
        pair_copy(1, part).wait_send()
    for copy in started:
        copy.wait_send()


def on_device(sizes, deviation, courant, collide, hole_cells, hole_wall, specular, specularity):
    width_x, width_y, block = deviation.shape
    cells = width_x * width_y
    n_space, n_row, n_col = sizes
    groups = n_row * n_col
    slots = hole_cells.shape[0]
    rows, piece = collide.shape
    vmem = pl.BlockSpec(memory_space=pltpu.VMEM)
    smem = pl.BlockSpec(memory_space=pltpu.SMEM)
    hbm = pl.BlockSpec(memory_space=pl.ANY)
    dma = pltpu.SemaphoreType.DMA
    sub = block // groups
    result = pl.pallas_call(
        functools.partial(body, sizes),
        out_shape=jax.ShapeDtypeStruct((cells, block), BF16),
        in_specs=[hbm, vmem, hbm, vmem, vmem, hbm, smem],
        out_specs=hbm,
        scratch_shapes=[
            pltpu.VMEM((cells, block), BF16),
            pltpu.VMEM((specular.shape[0], block), jnp.int32),
            pltpu.VMEM((width_x, width_y, block), BF16),
            pltpu.VMEM((n_row, cells, block), BF16),
            pltpu.VMEM((n_space, rows, piece), BF16),
            pltpu.VMEM((cells, block), F32),
            pltpu.VMEM((cells, block), BF16),
            pltpu.VMEM((2, width_y, block), BF16),
            pltpu.VMEM((groups, sub + 16, slots), BF16),
            pltpu.VMEM((groups, sub + 16, slots), BF16),
            pltpu.VMEM((2, cells, block), F32),
            pltpu.VMEM((2, cells, block), F32),
            pltpu.VMEM((cells, block), BF16),
            pltpu.VMEM((cells, block), BF16),
            dma((8,)),
            dma((8 * (n_space // 4),)),
            dma((8,)),
            dma((8,)),
            dma((2,)),
            dma((2,)),
            dma(()),
            dma(()),
            dma((CHUNKS,)),
            dma((2 * CHUNKS,)),
            dma((CHUNKS,)),
            dma((2 * CHUNKS,)),
            dma((CHUNKS,)),
            dma((CHUNKS,)),
            dma(()),
            dma(()),
            dma(()),
            dma(()),
        ],
        compiler_params=pltpu.CompilerParams(
            collective_id=0, has_side_effects=True, vmem_limit_bytes=60 * 2**20
        ),
        name="iterate",
    )(
        deviation,
        courant,
        collide,
        hole_cells,
        hole_wall,
        specular,
        specularity,
    )
    return result.reshape(width_x, width_y, block)


def solution(mesh):
    sizes = (mesh.shape["space"], mesh.shape["mrow"], mesh.shape["mcol"])
    in_specs = (
        P("space", None, ("mcol", "mrow")),
        P(None, ("mcol", "mrow")),
        P("mrow", ("mcol", "space")),
        P("space"),
        P("space"),
        P(),
        P(),
    )
    out_specs = P("space", None, ("mrow", "mcol"))
    return jax.shard_map(
        functools.partial(on_device, sizes),
        mesh=mesh,
        in_specs=in_specs,
        out_specs=out_specs,
        check_vma=False,
    )
```
